32 devices in a mesh: dp: 8 (over y, x, core), tensor: 4 (over z).
Axes of the slice: x: 2, y: 2, z: 4, core: 2. Of those that a mesh axis runs over, the one named last changes fastest.
Arguments:
- clips: bfloat16 [16, 1568, 768], P('dp', 'tensor'), may hold values from -6 to 6
- clip_live: int32 [16], P('dp'), may hold values 0 or 1
- qkv_weight: bfloat16 [2, 768, 3, 768], P(None, 'dp', None, 'tensor'), may hold values from -0.21875 to 0.21875
- proj_weight: bfloat16 [2, 768, 768], P(None, 'tensor', 'dp'), may hold values from -2.236068 to 2.236068
- fc1_weight: bfloat16 [768, 3072], P('dp', 'tensor'), may hold values from -0.21875 to 0.21875
- fc2_weight: bfloat16 [3072, 768], P('tensor', 'dp'), may hold values from -0.109375 to 0.109375
- attn_bias: bfloat16 [2, 2, 12, 64], P(None, None, 'tensor', 'dp'), may hold values from -3 to 3
- fc1_bias: bfloat16 [4, 768], P('tensor', 'dp'), may hold values from -3 to 3
- norm_params: bfloat16 [3, 2, 768], P(None, None, ('dp', 'tensor')), may hold values from -1.2 to 1.6
- tfc_weight: bfloat16 [768, 768], P(('dp', 'tensor')), may hold values from -0.21875 to 0.21875
- out_bias: bfloat16 [4, 768], P(None, ('dp', 'tensor')), may hold values from -2 to 2
- cotangent: bfloat16 [16, 1568, 768], P('dp', 'tensor'), may hold values from -6 to 6
Outputs:
- outputs: bfloat16 [16, 1568, 768], P('dp', 'tensor')
- grad_clips: float32 [16, 1568, 768], P('dp', 'tensor')
- grad_qkv: float32 [2, 768, 3, 768], P(None, 'dp', None, 'tensor')
- grad_proj: float32 [2, 768, 768], P(None, 'tensor', 'dp')
- grad_fc1: float32 [768, 3072], P('dp', 'tensor')
- grad_fc2: float32 [3072, 768], P('tensor', 'dp')
- grad_attn_bias: float32 [2, 2, 12, 64], P(None, None, 'tensor', 'dp')
- grad_fc1_bias: float32 [4, 768], P('tensor', 'dp')
- grad_norm: float32 [3, 2, 768], P(None, None, ('dp', 'tensor'))
- grad_tfc: float32 [768, 768], P(('dp', 'tensor'))
- grad_out_bias: float32 [4, 768], P(None, ('dp', 'tensor'))
The draws below stay inside these ranges and needn't reach their ends.
Inputs may be any that keep to these rules, and one draw needn't show every extreme that they name: `clip_live`: 1 where the slot holds a clip, 0 where it is empty.
All inputs are finite; a program needn't handle non-finite values. No bound on the sum of `clip_live` on one device may be relied on, other than what follows from the above.
Results may differ from the reference program's by a relative error of at most 0.034.
Values may be sent and summed in bfloat16 or wider, within the bound.
No kernel may reach another device: no remote copies, remote signals or barrier semaphores. Data moves between devices by JAX's collectives and lax.ppermute only.
A program may use at most 192 MiB of HBM per device.

```python
import jax
import jax.numpy as jnp
from jax import lax

D = 768
HEADS = 12
HD = 64
FF = 3072
FRAMES = 8
PATCHES = 196
TOKC = 1568
CLIPS = 16


def draw_proj_weight(key, part):
    noise = jnp.clip(jax.random.normal(key, (2, D, D), jnp.float32), -6.0, 6.0)
    scales = jnp.array([(FRAMES / (2.0 * D)) ** 0.5, (PATCHES / (2.0 * D)) ** 0.5], jnp.float32)
    return (noise * scales[:, None, None]).astype(jnp.bfloat16)


def draw_norm_params(key, part):
    noise = jnp.clip(jax.random.normal(key, (3, 2, D), jnp.float32), -4.0, 4.0)
    offset = jnp.array([1.0, 0.0], jnp.float32)[None, :, None]
    spread = jnp.array([0.15, 0.3], jnp.float32)[None, :, None]
    return (offset + spread * noise).astype(jnp.bfloat16)


def place_ends(entries, own_key, low, largest):
    longest = entries.shape.index(max(entries.shape))
    spots = []
    for shift in (0, 1):
        where = [jax.random.randint(jax.random.fold_in(own_key, axis), (), 0, length) for axis, length in enumerate(entries.shape)]
        where[longest] = (where[longest] + shift) % entries.shape[longest]
        spots.append(tuple(where))
    return entries.at[spots[0]].set(low).at[spots[1]].set(largest)


def levels(rng, dims, pieces, smallest, top_value):
    loudness = 1.0
    for axis_at, blocks in pieces:
        draws = jax.random.uniform(jax.random.fold_in(jax.random.fold_in(rng, 6), axis_at), (blocks,), jnp.float32, smallest / len(pieces), top_value / len(pieces))
        loudness = loudness * jnp.repeat(jnp.exp(draws), dims[axis_at] // blocks).reshape((-1,) + (1,) * (len(dims) - 1 - axis_at))
    return loudness


def bell_draw(own_key, extent, scale, bound, pieces=(), dtype=jnp.bfloat16):
    result = jax.random.normal(own_key, extent, jnp.float32) * scale
    if len(pieces) > 0:
        result = levels(own_key, extent, pieces, -0.22, 0.18) * result
    return jnp.clip(result, min=-bound, max=bound).astype(dtype)


def setup_inputs(seed: int = 0) -> dict:
    splits = jax.random.split(jax.random.key(seed), 13)
    return {
        "clips": bell_draw(splits[0], (CLIPS, TOKC, D), 1.0, 6.0, ((0, 8), (1, 4))),
        "clip_live": place_ends((jax.random.randint(splits[1], (CLIPS,), 0, 4) < 3).astype(jnp.int32), jax.random.fold_in(splits[1], 1), 0, 1),
        "qkv_weight": bell_draw(splits[2], (2, D, 3, D), D ** -0.5, 0.21875, ((1, 8), (3, 4))),
        "proj_weight": draw_proj_weight(jax.random.fold_in(splits[12], 71), 0),
        "fc1_weight": bell_draw(splits[4], (D, FF), D ** -0.5, 0.21875, ((0, 8), (1, 4))),
        "fc2_weight": bell_draw(splits[5], (FF, D), FF ** -0.5, 0.109375, ((0, 4), (1, 8))),
        "attn_bias": bell_draw(splits[6], (2, 2, HEADS, HD), 0.5, 3.0, ((2, 4), (3, 8))),
        "fc1_bias": bell_draw(splits[7], (FF // D, D), 0.5, 3.0, ((0, 4), (1, 8))),
        "norm_params": draw_norm_params(jax.random.fold_in(splits[12], 71), 0),
        "tfc_weight": bell_draw(splits[9], (D, D), D ** -0.5, 0.21875, ((0, 32),)),
        "out_bias": bell_draw(splits[10], (4, D), 0.3, 2.0, ((1, 32),)),
        "cotangent": bell_draw(splits[11], (CLIPS, TOKC, D), 1.0, 6.0, ((0, 8), (1, 4))),
    }


EPS = 1e-06

@jax.custom_vjp
def low(v):
    return lax.optimization_barrier(v.astype(jnp.bfloat16)).astype(jnp.float32)

@jax.custom_vjp
def low_back(v):
    return v

def low_keep(v):
    return (low(v), None)

def low_pass(kept, grad):
    return (grad,)

def back_keep(v):
    return (v, None)

def back_low(kept, grad):
    return (low(grad),)
low.defvjp(low_keep, low_pass)
low_back.defvjp(back_keep, back_low)

def layer_norm(inputs, norm_gain, norm_shift):
    average = lax.optimization_barrier(jnp.mean(inputs, axis=-1, keepdims=True))
    centred = inputs - average
    variance = lax.optimization_barrier(jnp.mean(centred * centred, axis=-1, keepdims=True))
    return centred * lax.rsqrt(variance + EPS) * norm_gain + norm_shift

def attention_core(query, keys, values, spatial):
    highest = lax.Precision.HIGHEST
    if spatial:
        scores = jnp.einsum('fphd,fqhd->hfpq', query, keys, precision=highest)
    else:
        scores = jnp.einsum('fphd,gphd->hpfg', query, keys, precision=highest)
    scores = low_back(scores * HD ** (-0.5))
    probs = low(jax.nn.softmax(scores, axis=-1))
    if spatial:
        heads = jnp.einsum('hfpq,fqhd->fphd', probs, values, precision=highest)
    else:
        heads = jnp.einsum('hpfg,gphd->fphd', probs, values, precision=highest)
    return low(low_back(heads.reshape(FRAMES * PATCHES, D)))

def clip_forward(inputs, params):
    qkv_w, proj_w, fc1_w, fc2_w, attn_b, fc1_b, norms, tfc_w, out_b = params
    highest = lax.Precision.HIGHEST

    def heads_branch(residual, branch):
        normed = low(layer_norm(residual, norms[branch, 0], norms[branch, 1]))
        mixed = jnp.einsum('nd,dke->nke', normed, qkv_w[branch], precision=highest)
        biases = attn_b[branch].reshape(2, D)
        mixed = mixed + jnp.stack([biases[0], jnp.zeros_like(biases[0]), biases[1]])
        mixed = low(low_back(mixed)).reshape(FRAMES, PATCHES, 3, HEADS, HD)
        heads = attention_core(mixed[:, :, 0], mixed[:, :, 1], mixed[:, :, 2], branch == 1)
        return jnp.dot(heads, proj_w[branch], precision=highest) + out_b[2 * branch]
    summed = low(low_back(heads_branch(inputs, 0)))
    first = inputs + low_back(jnp.dot(summed, tfc_w, precision=highest) + out_b[1])
    second = first + low_back(heads_branch(first, 1))
    normed = low(layer_norm(second, norms[2, 0], norms[2, 1]))
    hidden = low_back(jnp.dot(normed, fc1_w, precision=highest) + fc1_b.reshape(FF))
    active = low(jax.nn.gelu(hidden, approximate=False))
    return second + low_back(jnp.dot(active, fc2_w, precision=highest) + out_b[3])

def reference(clips, clip_live, qkv_weight, proj_weight, fc1_weight, fc2_weight, attn_bias, fc1_bias, norm_params, tfc_weight, out_bias, cotangent):
    params = tuple((item.astype(jnp.float32) for item in (qkv_weight, proj_weight, fc1_weight, fc2_weight, attn_bias, fc1_bias, norm_params, tfc_weight, out_bias)))
    inputs = clips.astype(jnp.float32)
    live = clip_live.astype(jnp.float32)[:, None, None]
    stepper = jax.checkpoint(clip_forward)

    def forward(values_in, weights):

        def one_clip(single):
            return stepper(single, weights)
        return lax.map(one_clip, values_in) * live
    outputs, pullback = jax.vjp(forward, inputs, params)
    grad_inputs, grads = pullback(cotangent.astype(jnp.float32))
    return (outputs.astype(jnp.bfloat16), grad_inputs, grads[0], grads[1], grads[2], grads[3], grads[4], grads[5], grads[6], grads[7], grads[8])
```

```python
from functools import partial

import jax
import jax.numpy as jnp
from jax import lax
from jax.experimental import pallas as pl
from jax.experimental.pallas import tpu as pltpu
from jax.sharding import PartitionSpec as P

FRAMES = 8
EPS = 1e-06
LOW = jnp.bfloat16
F32 = jnp.float32
NEG = -1e30


def dot_nn(left, right):
    return lax.dot_general(left, right, (((1,), (0,)), ((), ())), preferred_element_type=F32)


def dot_nt(left, right):
    return lax.dot_general(left, right, (((1,), (1,)), ((), ())), preferred_element_type=F32)


def dot_tn(left, right):
    return lax.dot_general(left, right, (((0,), (0,)), ((), ())), preferred_element_type=F32)


def line_moves(count):
    up = [(i, i + 1) for i in range(count - 1)]
    return up, [(b, a) for a, b in up]


def line_gather(block):
    count = lax.axis_size("tensor")
    place = lax.axis_index("tensor")
    up, down = line_moves(count)
    below, above = [block], [block]
    for _ in range(count - 1):
        below.append(lax.ppermute(below[-1], "tensor", up))
        above.append(lax.ppermute(above[-1], "tensor", down))
    back = [block] + [
        jnp.where(place >= k, below[k], above[count - k]) for k in range(1, count)
    ]
    ring = jnp.stack([back[(-j) % count] for j in range(count)] * 2)
    return lax.dynamic_slice_in_dim(ring, count - place, count, axis=0)


def line_scatter(blocks):
    count = lax.axis_size("tensor")
    place = lax.axis_index("tensor")
    up, down = line_moves(count)
    ahead = [
        lax.dynamic_index_in_dim(blocks, lax.rem(place + k, count), axis=0, keepdims=False)
        for k in range(count)
    ]
    zero = jnp.zeros_like(ahead[0])
    rise = [jnp.where(place + k < count, ahead[k], zero) for k in range(1, count)]
    fall = [jnp.where(place >= k, ahead[count - k], zero) for k in range(1, count)]
    sums = []
    for parts, moves in ((rise, up), (fall, down)):
        held = parts[-1]
        for k in range(count - 2, -1, -1):
            arrived = lax.ppermute(held, "tensor", moves)
            held = (parts[k].astype(F32) + arrived.astype(F32)).astype(LOW)
        sums.append(lax.ppermute(held, "tensor", moves))
    return ahead[0].astype(F32) + sums[0].astype(F32) + sums[1].astype(F32)


def swap_blocks(blocks, sign):
    count = lax.axis_size("tensor")
    moved = [blocks[0]]
    for k in range(1, count):
        pairs = [(i, (i + sign * k) % count) for i in range(count)]
        moved.append(lax.ppermute(blocks[k], "tensor", pairs))
    return jnp.concatenate(moved, axis=0)


def pair_lanes(rows):
    lane = lax.broadcasted_iota(jnp.int32, (rows, 128), 1)
    return lane < 64


def allowed(rows, group, keys):
    row = lax.broadcasted_iota(jnp.int32, (rows, rows), 0)
    col = lax.broadcasted_iota(jnp.int32, (rows, rows), 1)
    if keys is not None:
        return col < keys
    return (row // group) == (col // group)


def softmax_rows(query, keys, mask):
    scores = dot_nt(query, keys) * 0.125
    scores = jnp.where(mask, scores, NEG)
    top = jnp.max(scores, axis=-1, keepdims=True)
    grown = jnp.exp(scores - top)
    return grown / jnp.sum(grown, axis=-1, keepdims=True)


def attend_kernel(group, keys, width, mixed_ref, out_ref):
    rows = out_ref.shape[-2]
    mask = allowed(rows, group, keys)
    first = pair_lanes(rows)

    def pair(index, carry):
        at = pl.multiple_of(index * 128, 128)
        query = mixed_ref[:, pl.ds(at, 128)]
        key = mixed_ref[:, pl.ds(width + at, 128)]
        value = mixed_ref[:, pl.ds(2 * width + at, 128)]
        zero = jnp.zeros_like(query)
        total = jnp.zeros((rows, 128), F32)
        for side in (first, jnp.logical_not(first)):
            probs = softmax_rows(query, jnp.where(side, key, zero), mask).astype(LOW)
            total = total + dot_nn(probs, jnp.where(side, value, zero))
        out_ref[:, pl.ds(at, 128)] = total.astype(LOW)
        return carry

    lax.fori_loop(0, width // 128, pair, 0)


def attend_back_kernel(group, keys, width, mixed_ref, grad_ref, out_ref):
    rows = grad_ref.shape[-2]
    mask = allowed(rows, group, keys)
    first = pair_lanes(rows)

    def pair(index, carry):
        at = pl.multiple_of(index * 128, 128)
        query = mixed_ref[:, pl.ds(at, 128)]
        key = mixed_ref[:, pl.ds(width + at, 128)]
        value = mixed_ref[:, pl.ds(2 * width + at, 128)]
        grad = grad_ref[:, pl.ds(at, 128)]
        zero = jnp.zeros_like(query)
        dq = jnp.zeros((rows, 128), F32)
        dk = jnp.zeros((rows, 128), F32)
        dv = jnp.zeros((rows, 128), F32)
        for side in (first, jnp.logical_not(first)):
            key_side = jnp.where(side, key, zero)
            probs = softmax_rows(query, key_side, mask)
            grad_probs = dot_nt(grad, jnp.where(side, value, zero))
            inner = jnp.sum(grad_probs * probs, axis=-1, keepdims=True)
            grad_scores = ((probs * (grad_probs - inner)).astype(LOW)) * 0.125
            grad_scores = grad_scores.astype(LOW)
            dv = dv + dot_tn(probs.astype(LOW), jnp.where(side, grad, zero))
            dq = dq + dot_nn(grad_scores, key_side)
            dk = dk + dot_tn(grad_scores, jnp.where(side, query, zero))
        out_ref[:, pl.ds(at, 128)] = dq.astype(LOW)
        out_ref[:, pl.ds(width + at, 128)] = dk.astype(LOW)
        out_ref[:, pl.ds(2 * width + at, 128)] = dv.astype(LOW)
        return carry

    lax.fori_loop(0, width // 128, pair, 0)


def attend(mixed, blocks, rows, group, keys):
    width = mixed.shape[1] // 3
    out = pl.pallas_call(
        partial(attend_kernel, group, keys, width),
        grid=(blocks,),
        in_specs=[pl.BlockSpec((None, rows, 3 * width), lambda i: (i, 0, 0))],
        out_specs=pl.BlockSpec((None, rows, width), lambda i: (i, 0, 0)),
        out_shape=jax.ShapeDtypeStruct((blocks, rows, width), LOW),
        compiler_params=pltpu.CompilerParams(vmem_limit_bytes=32 << 20),
        name="attend",
    )(mixed.reshape(blocks, rows, 3 * width))
    return out.reshape(blocks * rows, width)


def attend_back(mixed, grad, blocks, rows, group, keys):
    width = grad.shape[1]
    out = pl.pallas_call(
        partial(attend_back_kernel, group, keys, width),
        grid=(blocks,),
        in_specs=[
            pl.BlockSpec((None, rows, 3 * width), lambda i: (i, 0, 0)),
            pl.BlockSpec((None, rows, width), lambda i: (i, 0, 0)),
        ],
        out_specs=pl.BlockSpec((None, rows, 3 * width), lambda i: (i, 0, 0)),
        out_shape=jax.ShapeDtypeStruct((blocks, rows, 3 * width), LOW),
        compiler_params=pltpu.CompilerParams(vmem_limit_bytes=32 << 20),
        name="attend_back",
    )(mixed.reshape(blocks, rows, 3 * width), grad.reshape(blocks, rows, width))
    return out.reshape(blocks * rows, 3 * width)


def norm_stats(rows):
    centred = rows - jnp.mean(rows, axis=-1, keepdims=True)
    scale = lax.rsqrt(jnp.mean(centred * centred, axis=-1, keepdims=True) + EPS)
    return centred * scale, scale


def norm_low(rows, gain, shift):
    return (norm_stats(rows)[0] * gain + shift).astype(LOW)


def norm_back(grad, rows, gain):
    unit, scale = norm_stats(rows)
    scaled = grad * gain
    mean_plain = jnp.mean(scaled, axis=-1, keepdims=True)
    mean_unit = jnp.mean(scaled * unit, axis=-1, keepdims=True)
    back = (scaled - mean_plain - unit * mean_unit) * scale
    return back, jnp.sum(grad * unit, axis=0), jnp.sum(grad, axis=0)


def column_sums(rows):
    return jnp.sum(rows.astype(F32), axis=0)


def gelu_parts(hidden):
    cdf = 0.5 * (1.0 + lax.erf(hidden * (2.0**-0.5)))
    return cdf


def gelu_slope(hidden):
    density = jnp.exp(-0.5 * hidden * hidden) * 0.3989422804014327
    return gelu_parts(hidden) + hidden * density


def shards(
    clips,
    clip_live,
    qkv_weight,
    proj_weight,
    fc1_weight,
    fc2_weight,
    attn_bias,
    fc1_bias,
    norm_params,
    tfc_weight,
    out_bias,
    cotangent,
):
    tp = lax.axis_size("tensor")
    place = lax.axis_index("tensor")
    slots, tokens, width = clips.shape
    part = qkv_weight.shape[3]
    drow = qkv_weight.shape[1]
    srow = tfc_weight.shape[0]
    hidden_part = fc1_weight.shape[1]
    frames = FRAMES // tp
    patches = tokens // frames
    share = patches // tp
    padded = -(-patches // 8) * 8
    images = slots * frames
    rows_f = images * padded
    group_rows = images * share
    block_rows = -(-group_rows // 8) * 8
    rows_t = slots * share * FRAMES

    small = jnp.concatenate(
        [
            norm_params.reshape(6, srow).T,
            out_bias.T,
            attn_bias.reshape(4, srow).T,
            fc1_bias.reshape(tp, srow).T,
        ],
        axis=1,
    )
    small_cols = small.shape[1]
    shared_cols = width + 256
    shared = jnp.concatenate(
        [tfc_weight, jnp.pad(small, ((0, 0), (0, 256 - small_cols)))], axis=1
    ).reshape(drow, shared_cols // tp)

    def branch_rows(both):
        qkv = both[:, :, : 3 * part].reshape(tp, drow, 3, part)
        proj = both[:, :, 3 * part : 4 * part]
        return [
            qkv.transpose(1, 2, 0, 3).reshape(drow, 3 * width),
            proj.transpose(1, 0, 2).reshape(drow, width),
        ]

    def spread(rows):
        return lax.all_gather(rows, "dp", axis=0, tiled=True)

    gathered = line_gather(
        jnp.concatenate([qkv_weight[0].reshape(drow, 3 * part), proj_weight[0].T, shared], axis=1)
    )
    shared_rows = gathered[:, :, 4 * part :].reshape(drow, shared_cols)
    time_all = spread(jnp.concatenate(branch_rows(gathered) + [shared_rows], axis=1))
    gathered = line_gather(
        jnp.concatenate([qkv_weight[1].reshape(drow, 3 * part), proj_weight[1].T], axis=1)
    )
    space_all = spread(jnp.concatenate(branch_rows(gathered), axis=1))
    gathered = line_gather(jnp.concatenate([fc1_weight, fc2_weight.T], axis=1))
    mlp_all = spread(
        jnp.concatenate(
            [
                gathered[:, :, :hidden_part].transpose(1, 0, 2).reshape(drow, tp * hidden_part),
                gathered[:, :, hidden_part:].transpose(1, 0, 2).reshape(drow, tp * hidden_part),
            ],
            axis=1,
        )
    )
    qkv_w = (time_all[:, : 3 * width], space_all[:, : 3 * width])
    proj_w = (time_all[:, 3 * width : 4 * width], space_all[:, 3 * width :])
    tfc_w = time_all[:, 4 * width : 5 * width]
    fc1_w = mlp_all[:, : tp * hidden_part]
    fc2_w = mlp_all[:, tp * hidden_part :]
    small_all = time_all[:, 5 * width : 5 * width + small_cols].astype(F32).T
    norms = small_all[:6].reshape(3, 2, width)
    out_b = small_all[6:10]
    dp = width // drow
    heads_local = attn_bias.shape[2]
    attn_b = (
        small_all[10:14]
        .reshape(2, 2, dp, tp, heads_local, -1)
        .transpose(0, 1, 3, 4, 2, 5)
        .reshape(2, 2, width)
    )
    hidden_b = (
        small_all[14 : 14 + tp].reshape(tp, dp, tp, srow).transpose(2, 1, 0, 3).reshape(-1)
    )
    bias_rows = [
        jnp.concatenate([attn_b[b, 0], jnp.zeros((width,), F32), attn_b[b, 1]]) for b in (0, 1)
    ]

    row = lax.broadcasted_iota(jnp.int32, (tp, block_rows, images, padded), 1)
    shift = lax.broadcasted_iota(jnp.int32, (tp, block_rows, images, padded), 0)
    image = lax.broadcasted_iota(jnp.int32, (tp, block_rows, images, padded), 2)
    patch = lax.broadcasted_iota(jnp.int32, (tp, block_rows, images, padded), 3)
    target = lax.rem(place + shift, tp)
    pick = ((row // share) == image) & ((row % share) + target * share == patch)
    pick = (pick & (row < group_rows)).astype(LOW).reshape(tp * block_rows, rows_f)
    row = lax.broadcasted_iota(jnp.int32, (rows_t, tp, block_rows), 0)
    shift = lax.broadcasted_iota(jnp.int32, (rows_t, tp, block_rows), 1)
    sent = lax.broadcasted_iota(jnp.int32, (rows_t, tp, block_rows), 2)
    source = lax.rem(place - shift + tp, tp)
    frame = row % FRAMES
    merge = (frame // frames) == source
    merge = merge & (
        ((row // (FRAMES * share)) * frames + frame % frames) * share + (row // FRAMES) % share
        == sent
    )
    merge = merge.astype(LOW).reshape(rows_t, tp * block_rows)

    def cut(rows):
        return [rows[k * block_rows : (k + 1) * block_rows] for k in range(tp)]

    def to_patches(rows):
        sent = dot_nn(pick, rows).astype(LOW)
        return dot_nn(merge, swap_blocks(cut(sent), 1))

    def to_frames(rows):
        sent = dot_tn(merge, rows).astype(LOW)
        return dot_tn(pick, swap_blocks(cut(sent), -1))

    def pad_rows(values):
        shaped = values.reshape(images, patches, width)
        return jnp.pad(shaped, ((0, 0), (0, padded - patches), (0, 0))).reshape(rows_f, width)

    def drop_rows(values):
        return values.reshape(images, padded, width)[:, :patches].reshape(slots, tokens, width)

    inputs_low = pad_rows(clips)
    live = jnp.repeat(clip_live.astype(F32), frames * padded)[:, None]

    def qkv_of(normed, b):
        return (dot_nn(normed, qkv_w[b]) + bias_rows[b]).astype(LOW)

    time_core = (rows_t // 112, 112, FRAMES, None)
    space_core = (images, padded, None, patches)

    inputs_t = to_patches(inputs_low)
    n1 = norm_low(inputs_t, norms[0, 0], norms[0, 1])
    mixed_t = qkv_of(n1, 0)
    heads_t = attend(mixed_t, *time_core)
    summed = (dot_nt(heads_t, proj_w[0]) + out_b[0]).astype(LOW)
    moved = (dot_nn(summed, tfc_w) + out_b[1]).astype(LOW)
    first = inputs_low.astype(F32) + to_frames(moved)
    n2 = norm_low(first, norms[1, 0], norms[1, 1])
    mixed_s = qkv_of(n2, 1)
    heads_s = attend(mixed_s, *space_core)
    second = first + dot_nt(heads_s, proj_w[1]) + out_b[2]
    n3 = norm_low(second, norms[2, 0], norms[2, 1])
    hidden = dot_nn(n3, fc1_w) + hidden_b
    active = (hidden * gelu_parts(hidden)).astype(LOW)
    result = second + dot_nt(active, fc2_w) + out_b[3]
    outputs = drop_rows((result * live).astype(LOW))

    grad_result = pad_rows(cotangent).astype(F32) * live
    grad_low = grad_result.astype(LOW)
    grad_fc2 = dot_tn(grad_low, active).astype(LOW)
    grad_hidden = (dot_nn(grad_low, fc2_w) * gelu_slope(hidden)).astype(LOW)
    grad_fc1 = dot_tn(n3, grad_hidden).astype(LOW)
    grad_n3 = dot_nt(grad_hidden, fc1_w)
    back, gain_m, shift_m = norm_back(grad_n3, second, norms[2, 0])
    grad_second = grad_result + back

    def branch_back(low, mixed, heads, normed, b, core):
        grad_proj = dot_tn(low, heads).astype(LOW)
        grad_heads = dot_nn(low, proj_w[b]).astype(LOW)
        grad_mixed = attend_back(mixed, grad_heads, *core)
        grad_qkv = dot_tn(normed, grad_mixed).astype(LOW)
        sums = column_sums(grad_mixed)
        grad_normed = dot_nt(grad_mixed, qkv_w[b])
        return grad_normed, grad_qkv, grad_proj, sums

    low_s = grad_second.astype(LOW)
    grad_n2, qkv_s, proj_s, sums_s = branch_back(low_s, mixed_s, heads_s, n2, 1, space_core)
    back, gain_s, shift_s = norm_back(grad_n2, first, norms[1, 0])
    grad_first = grad_second + back
    low_f = to_patches(grad_first.astype(LOW)).astype(LOW)
    grad_tfc = dot_tn(summed, low_f).astype(LOW)
    low_t = dot_nt(low_f, tfc_w).astype(LOW)
    grad_n1, qkv_t, proj_t, sums_t = branch_back(low_t, mixed_t, heads_t, n1, 0, time_core)
    back, gain_t, shift_t = norm_back(grad_n1, inputs_t, norms[0, 0])
    grad_inputs = grad_first + to_frames(back.astype(LOW))
    grad_clips = drop_rows(grad_inputs)

    feature = jnp.stack(
        [
            gain_t,
            shift_t,
            gain_s,
            shift_s,
            gain_m,
            shift_m,
            column_sums(low_t),
            column_sums(low_f),
            column_sums(low_s),
            column_sums(grad_low),
        ]
    )
    attn_sums = jnp.stack(
        [sums_t[:width], sums_t[2 * width :], sums_s[:width], sums_s[2 * width :]]
    )
    attn_sums = (
        attn_sums.reshape(4, tp, heads_local, dp, -1).transpose(0, 3, 1, 2, 4).reshape(4, width)
    )
    hidden_sums = (
        column_sums(grad_hidden).reshape(tp, dp, tp, srow).transpose(2, 1, 0, 3).reshape(tp, width)
    )
    small_grad = jnp.concatenate([feature, attn_sums, hidden_sums]).astype(LOW)
    small_grad = jnp.pad(small_grad, ((0, 256 - small_cols), (0, 0))).T

    def collect(rows):
        return lax.psum_scatter(rows, "dp", scatter_dimension=0, tiled=True)

    def split_cols(rows, pieces):
        return rows.reshape(drow, pieces, tp, -1).transpose(2, 0, 1, 3)

    fc2_done = line_scatter(split_cols(collect(grad_fc2), 1))
    fc1_done = line_scatter(split_cols(collect(grad_fc1), 1))

    def branch_blocks(rows):
        return jnp.concatenate(
            [
                split_cols(rows[:, : 3 * width], 3).reshape(tp, drow, 3 * part),
                split_cols(rows[:, 3 * width : 4 * width], 1).reshape(tp, drow, part),
            ],
            axis=2,
        )

    space_done = line_scatter(branch_blocks(collect(jnp.concatenate([qkv_s, proj_s], axis=1))))
    time_rows = collect(jnp.concatenate([qkv_t, proj_t, grad_tfc, small_grad], axis=1))
    shared_back = time_rows[:, 4 * width :].reshape(tp, srow, shared_cols)
    time_done = line_scatter(
        jnp.concatenate(
            [branch_blocks(time_rows), shared_back.reshape(tp, drow, shared_cols // tp)], axis=2
        )
    )
    grad_qkv = jnp.stack([time_done[:, : 3 * part], space_done[:, : 3 * part]]).reshape(
        2, drow, 3, part
    )
    grad_proj = jnp.stack([time_done[:, 3 * part : 4 * part].T, space_done[:, 3 * part :].T])
    shared_done = time_done[:, 4 * part :].reshape(srow, shared_cols)
    smalls = shared_done[:, width : width + small_cols].T
    return (
        outputs,
        grad_clips,
        grad_qkv,
        grad_proj,
        fc1_done.reshape(drow, hidden_part),
        fc2_done.reshape(drow, hidden_part).T,
        smalls[10:14].reshape(attn_bias.shape),
        smalls[14 : 14 + tp].reshape(fc1_bias.shape),
        smalls[:6].reshape(3, 2, srow),
        shared_done[:, :width],
        smalls[6:10],
    )


def solution(mesh):
    return jax.shard_map(
        shards,
        mesh=mesh,
        in_specs=(
            P("dp", "tensor", None),
            P("dp"),
            P(None, "dp", None, "tensor"),
            P(None, "tensor", "dp"),
            P("dp", "tensor"),
            P("tensor", "dp"),
            P(None, None, "tensor", "dp"),
            P("tensor", "dp"),
            P(None, None, ("dp", "tensor")),
            P(("dp", "tensor"), None),
            P(None, ("dp", "tensor")),
            P("dp", "tensor", None),
        ),
        out_specs=(
            P("dp", "tensor", None),
            P("dp", "tensor", None),
            P(None, "dp", None, "tensor"),
            P(None, "tensor", "dp"),
            P("dp", "tensor"),
            P("tensor", "dp"),
            P(None, None, "tensor", "dp"),
            P("tensor", "dp"),
            P(None, None, ("dp", "tensor")),
            P(("dp", "tensor"), None),
            P(None, ("dp", "tensor")),
        ),
        check_vma=False,
    )
```

```python
from functools import partial

import jax
import jax.numpy as jnp
from jax import lax
from jax.experimental import pallas as pl
from jax.experimental.pallas import tpu as pltpu
from jax.sharding import PartitionSpec as P

FRAMES = 8
EPS = 1e-06
LOW = jnp.bfloat16
F32 = jnp.float32
NEG = -1e30


def dot_nn(left, right):
    return lax.dot_general(left, right, (((1,), (0,)), ((), ())), preferred_element_type=F32)


def dot_nt(left, right):
    return lax.dot_general(left, right, (((1,), (1,)), ((), ())), preferred_element_type=F32)


def dot_tn(left, right):
    return lax.dot_general(left, right, (((0,), (0,)), ((), ())), preferred_element_type=F32)


def line_shift(block, step):
    count = lax.axis_size("tensor")
    return lax.ppermute(block, "tensor", [(i, (i + step) % count) for i in range(count)])


def line_gather(block):
    return [block] + [line_shift(block, k) for k in range(1, lax.axis_size("tensor"))]


def line_order(back):
    count = lax.axis_size("tensor")
    ring = jnp.stack([back[(-j) % count] for j in range(count)] * 2)
    return lax.dynamic_slice_in_dim(ring, count - lax.axis_index("tensor"), count, axis=0)


def line_scatter(blocks):
    count = lax.axis_size("tensor")
    place = lax.axis_index("tensor")
    parts = []
    for k in range(count):
        ahead = lax.dynamic_index_in_dim(
            blocks, lax.rem(place + k, count), axis=0, keepdims=False
        )
        parts.append(ahead if k == 0 else line_shift(ahead, k))
    return parts


def line_total(parts):
    total = parts[0].astype(F32)
    for part in parts[1:]:
        total = total + part.astype(F32)
    return total


def swap_blocks(blocks, sign):
    count = lax.axis_size("tensor")
    moved = [blocks[0]]
    for k in range(1, count):
        pairs = [(i, (i + sign * k) % count) for i in range(count)]
        moved.append(lax.ppermute(blocks[k], "tensor", pairs))
    return jnp.concatenate(moved, axis=0)


def pair_sides(values, first):
    wide = values.astype(F32)
    zero = jnp.zeros_like(wide)
    both = [jnp.where(first, wide, zero), jnp.where(first, zero, wide)]
    return jnp.concatenate(both, axis=0).astype(LOW)


def key_mask(rows, group, keys):
    key = lax.broadcasted_iota(jnp.int32, (2, rows, rows), 1)
    query = lax.broadcasted_iota(jnp.int32, (2, rows, rows), 2)
    if keys is not None:
        return key < keys
    return (key // group) == (query // group)


def pair_probs(query, key_sides, mask, rows):
    scores = dot_nt(key_sides, query).reshape(2, rows, rows)
    scores = jnp.where(mask, scores, NEG)
    grown = jnp.exp(scores - jnp.max(scores, axis=1, keepdims=True))
    return grown * (1.0 / jnp.sum(grown, axis=1, keepdims=True))


def attend_kernel(group, keys, width, mixed_ref, out_ref):
    rows = out_ref.shape[-2]
    mask = key_mask(rows, group, keys)
    first = lax.broadcasted_iota(jnp.int32, (rows, 128), 1) < 64
    for at in range(0, width, 128):
        query = mixed_ref[:, at : at + 128] * LOW(0.125)
        key = pair_sides(mixed_ref[:, width + at : width + at + 128], first)
        value = pair_sides(mixed_ref[:, 2 * width + at : 2 * width + at + 128], first)
        probs = pair_probs(query, key, mask, rows).reshape(2 * rows, rows)
        out_ref[:, at : at + 128] = dot_tn(probs.astype(LOW), value).astype(LOW)


def attend_back_kernel(group, keys, width, mixed_ref, grad_ref, out_ref, sums_ref):
    rows = grad_ref.shape[-2]
    mask = key_mask(rows, group, keys)
    first = lax.broadcasted_iota(jnp.int32, (rows, 128), 1) < 64

    @pl.when(pl.program_id(0) == 0)
    def clear():
        sums_ref[...] = jnp.zeros_like(sums_ref)

    for at in range(0, width, 128):
        query = mixed_ref[:, at : at + 128] * LOW(0.125)
        key = pair_sides(mixed_ref[:, width + at : width + at + 128], first)
        value = pair_sides(mixed_ref[:, 2 * width + at : 2 * width + at + 128], first)
        grad = grad_ref[:, at : at + 128]
        probs = pair_probs(query, key, mask, rows)
        grad_probs = dot_nt(value, grad).reshape(2, rows, rows)
        inner = jnp.sum(grad_probs * probs, axis=1, keepdims=True)
        grad_scores = (probs * (grad_probs - inner)).reshape(2 * rows, rows).astype(LOW)
        probs_low = probs.reshape(2 * rows, rows).astype(LOW)
        dq = (dot_tn(grad_scores, key) * 0.125).astype(LOW)
        dk = dot_nn(grad_scores, query)
        dv = dot_nn(probs_low, grad)
        dk = jnp.where(first, dk[:rows], dk[rows:]).astype(LOW)
        dv = jnp.where(first, dv[:rows], dv[rows:]).astype(LOW)
        out_ref[:, at : at + 128] = dq
        out_ref[:, width + at : width + at + 128] = dk
        out_ref[:, 2 * width + at : 2 * width + at + 128] = dv
        for part, value in ((0, dq), (2, dv)):
            start = part * width + at
            total = jnp.sum(value.astype(F32), axis=0, keepdims=True)
            sums_ref[:, start : start + 128] = sums_ref[:, start : start + 128] + total


def attend(mixed, blocks, rows, group, keys):
    width = mixed.shape[1] // 3
    out = pl.pallas_call(
        partial(attend_kernel, group, keys, width),
        grid=(blocks,),
        in_specs=[pl.BlockSpec((None, rows, 3 * width), lambda i: (i, 0, 0))],
        out_specs=pl.BlockSpec((None, rows, width), lambda i: (i, 0, 0)),
        out_shape=jax.ShapeDtypeStruct((blocks, rows, width), LOW),
        compiler_params=pltpu.CompilerParams(vmem_limit_bytes=32 << 20),
        cost_estimate=pl.CostEstimate(
            flops=8_000_000_000, bytes_accessed=8 * blocks * rows * width, transcendentals=0
        ),
        name="attend",
    )(mixed.reshape(blocks, rows, 3 * width))
    return out.reshape(blocks * rows, width)


def attend_back(mixed, grad, blocks, rows, group, keys):
    width = grad.shape[1]
    out, sums = pl.pallas_call(
        partial(attend_back_kernel, group, keys, width),
        grid=(blocks,),
        in_specs=[
            pl.BlockSpec((None, rows, 3 * width), lambda i: (i, 0, 0)),
            pl.BlockSpec((None, rows, width), lambda i: (i, 0, 0)),
        ],
        out_specs=[
            pl.BlockSpec((None, rows, 3 * width), lambda i: (i, 0, 0)),
            pl.BlockSpec((1, 3 * width), lambda i: (0, 0)),
        ],
        out_shape=[
            jax.ShapeDtypeStruct((blocks, rows, 3 * width), LOW),
            jax.ShapeDtypeStruct((1, 3 * width), F32),
        ],
        compiler_params=pltpu.CompilerParams(vmem_limit_bytes=32 << 20),
        cost_estimate=pl.CostEstimate(
            flops=18_000_000_000, bytes_accessed=14 * blocks * rows * width, transcendentals=0
        ),
        name="attend_back",
    )(mixed.reshape(blocks, rows, 3 * width), grad.reshape(blocks, rows, width))
    return out.reshape(blocks * rows, 3 * width), sums[0]


def norm_stats(rows):
    centred = rows - jnp.mean(rows, axis=-1, keepdims=True)
    scale = lax.rsqrt(jnp.mean(centred * centred, axis=-1, keepdims=True) + EPS)
    return centred * scale, scale


def norm_low(rows, gain, shift):
    return (norm_stats(rows)[0] * gain + shift).astype(LOW)


def norm_back(grad, rows, gain):
    unit, scale = norm_stats(rows)
    scaled = grad * gain
    mean_plain = jnp.mean(scaled, axis=-1, keepdims=True)
    mean_unit = jnp.mean(scaled * unit, axis=-1, keepdims=True)
    back = (scaled - mean_plain - unit * mean_unit) * scale
    return back, jnp.sum(grad * unit, axis=0), jnp.sum(grad, axis=0)


def column_sums(rows):
    return jnp.sum(rows.astype(F32), axis=0)


def together(*values):
    return lax.optimization_barrier(values)


def shards(
    clips,
    clip_live,
    qkv_weight,
    proj_weight,
    fc1_weight,
    fc2_weight,
    attn_bias,
    fc1_bias,
    norm_params,
    tfc_weight,
    out_bias,
    cotangent,
):
    tp = lax.axis_size("tensor")
    place = lax.axis_index("tensor")
    slots, tokens, width = clips.shape
    part = qkv_weight.shape[3]
    drow = qkv_weight.shape[1]
    srow = tfc_weight.shape[0]
    hidden_part = fc1_weight.shape[1]
    frames = FRAMES // tp
    patches = tokens // frames
    share = patches // tp
    padded = -(-patches // 8) * 8
    images = slots * frames
    rows_f = images * padded
    group_rows = images * share
    block_rows = -(-group_rows // 8) * 8
    rows_t = slots * share * FRAMES

    small = jnp.concatenate(
        [
            norm_params.reshape(6, srow).T,
            out_bias.T,
            attn_bias.reshape(4, srow).T,
            fc1_bias.reshape(tp, srow).T,
        ],
        axis=1,
    )
    small_cols = small.shape[1]
    shared_cols = width + 256
    shared = jnp.concatenate(
        [tfc_weight, jnp.pad(small, ((0, 0), (0, 256 - small_cols)))], axis=1
    ).reshape(drow, shared_cols // tp)

    def branch_rows(both):
        qkv = both[:, :, : 3 * part].reshape(tp, drow, 3, part)
        proj = both[:, :, 3 * part : 4 * part]
        return [
            qkv.transpose(1, 2, 0, 3).reshape(drow, 3 * width),
            proj.transpose(1, 0, 2).reshape(drow, width),
        ]

    def spread(rows):
        return lax.all_gather(rows, "dp", axis=0, tiled=True)

    def cut(rows):
        return [rows[k * block_rows : (k + 1) * block_rows] for k in range(tp)]

    def pick_rows(columns):
        dims = (tp, block_rows, images, columns)
        shift, row, image, patch = (lax.broadcasted_iota(jnp.int32, dims, d) for d in range(4))
        target = lax.rem(place + shift, tp)
        found = ((row // share) == image) & ((row % share) + target * share == patch)
        return (found & (row < group_rows)).astype(LOW).reshape(tp * block_rows, images * columns)

    pick = pick_rows(padded)
    pick_plain = pick_rows(patches)
    dims = (rows_t, tp, block_rows)
    row, shift, sent = (lax.broadcasted_iota(jnp.int32, dims, d) for d in range(3))
    frame = row % FRAMES
    merge = ((frame // frames) == lax.rem(place - shift + tp, tp)) & (
        ((row // (FRAMES * share)) * frames + frame % frames) * share + (row // FRAMES) % share
        == sent
    )
    merge = merge.astype(LOW).reshape(rows_t, tp * block_rows)

    time_own = jnp.concatenate(
        [qkv_weight[0].reshape(drow, 3 * part), proj_weight[0].T, shared], axis=1
    )
    space_own = jnp.concatenate([qkv_weight[1].reshape(drow, 3 * part), proj_weight[1].T], axis=1)
    mlp_own = jnp.concatenate([fc1_weight, fc2_weight.T], axis=1)
    sent_x = dot_nn(pick_plain, clips.reshape(slots * tokens, width)).astype(LOW)
    time_back = line_gather(time_own)
    *time_back, sent_x = together(*time_back, sent_x)
    came_x = swap_blocks(cut(sent_x), 1)
    space_own, sent_x = together(space_own, sent_x)
    space_back = line_gather(space_own)
    gathered = line_order(time_back)
    shared_rows = gathered[:, :, 4 * part :].reshape(drow, shared_cols)
    time_all = spread(jnp.concatenate(branch_rows(gathered) + [shared_rows], axis=1))
    mlp_own, came_x = together(mlp_own, came_x)
    mlp_back = line_gather(mlp_own)
    space_all = spread(jnp.concatenate(branch_rows(line_order(space_back)), axis=1))
    qkv_w = (time_all[:, : 3 * width], space_all[:, : 3 * width])
    proj_w = (time_all[:, 3 * width : 4 * width], space_all[:, 3 * width :])
    tfc_w = time_all[:, 4 * width : 5 * width]
    small_all = time_all[:, 5 * width : 5 * width + small_cols].astype(F32).T
    norms = small_all[:6].reshape(3, 2, width)
    out_b = small_all[6:10]
    dp = width // drow
    heads_local = attn_bias.shape[2]
    attn_b = (
        small_all[10:14]
        .reshape(2, 2, dp, tp, heads_local, -1)
        .transpose(0, 1, 3, 4, 2, 5)
        .reshape(2, 2, width)
    )
    hidden_b = (
        small_all[14 : 14 + tp].reshape(tp, dp, tp, srow).transpose(2, 1, 0, 3).reshape(-1)
    )
    bias_rows = [
        jnp.concatenate([attn_b[b, 0], jnp.zeros((width,), F32), attn_b[b, 1]]) for b in (0, 1)
    ]

    def to_patches(rows):
        sent = dot_nn(pick, rows).astype(LOW)
        return dot_nn(merge, swap_blocks(cut(sent), 1))

    def to_frames(rows):
        sent = dot_tn(merge, rows).astype(LOW)
        return dot_tn(pick, swap_blocks(cut(sent), -1))

    def pad_rows(values):
        shaped = values.reshape(images, patches, width)
        return jnp.pad(shaped, ((0, 0), (0, padded - patches), (0, 0))).reshape(rows_f, width)

    def drop_rows(values):
        return values.reshape(images, padded, width)[:, :patches].reshape(slots, tokens, width)

    inputs_low = pad_rows(clips)
    live = jnp.repeat(clip_live.astype(F32), frames * padded)[:, None]

    def qkv_of(normed, b):
        return (dot_nn(normed, qkv_w[b]) + bias_rows[b]).astype(LOW)

    time_blocks = 1
    while rows_t // time_blocks > 128 or rows_t % (8 * time_blocks):
        time_blocks += 1
    time_core = (time_blocks, rows_t // time_blocks, FRAMES, None)
    space_core = (images, padded, None, patches)

    inputs_t = dot_nn(merge, came_x)
    n1 = norm_low(inputs_t, norms[0, 0], norms[0, 1])
    mixed_t = qkv_of(n1, 0)
    heads_t = attend(mixed_t, *time_core)
    *mlp_back, heads_t = together(*mlp_back, heads_t)
    gathered = line_order(mlp_back)
    mlp_all = spread(
        jnp.concatenate(
            [
                gathered[:, :, :hidden_part].transpose(1, 0, 2).reshape(drow, tp * hidden_part),
                gathered[:, :, hidden_part:].transpose(1, 0, 2).reshape(drow, tp * hidden_part),
            ],
            axis=1,
        )
    )
    fc1_w = mlp_all[:, : tp * hidden_part]
    fc2_w = mlp_all[:, tp * hidden_part :]
    summed = (dot_nt(heads_t, proj_w[0]) + out_b[0]).astype(LOW)
    moved = (dot_nn(summed, tfc_w) + out_b[1]).astype(LOW)
    first = inputs_low.astype(F32) + to_frames(moved)
    n2 = norm_low(first, norms[1, 0], norms[1, 1])
    mixed_s = qkv_of(n2, 1)
    heads_s = attend(mixed_s, *space_core)
    second = first + dot_nt(heads_s, proj_w[1]) + out_b[2]
    n3 = norm_low(second, norms[2, 0], norms[2, 1])
    hidden = dot_nn(n3, fc1_w) + hidden_b
    cdf = 0.5 * (1.0 + lax.erf(hidden * (2.0**-0.5)))
    active = (hidden * cdf).astype(LOW)
    slope = (cdf + hidden * jnp.exp(-0.5 * hidden * hidden) * 0.3989422804014327).astype(LOW)
    result = second + dot_nt(active, fc2_w) + out_b[3]
    outputs = drop_rows((result * live).astype(LOW))

    grad_result = pad_rows(cotangent).astype(F32) * live
    grad_low = grad_result.astype(LOW)
    grad_fc2 = dot_tn(grad_low, active).astype(LOW)
    grad_hidden = (dot_nn(grad_low, fc2_w) * slope.astype(F32)).astype(LOW)
    grad_fc1 = dot_tn(n3, grad_hidden).astype(LOW)
    grad_n3 = dot_nt(grad_hidden, fc1_w)
    back, gain_m, shift_m = norm_back(grad_n3, second, norms[2, 0])
    grad_second = grad_result + back

    def branch_back(low, mixed, heads, normed, b, core):
        grad_proj = dot_tn(low, heads).astype(LOW)
        grad_heads = dot_nn(low, proj_w[b]).astype(LOW)
        grad_mixed, sums = attend_back(mixed, grad_heads, *core)
        grad_qkv = dot_tn(normed, grad_mixed).astype(LOW)
        grad_normed = dot_nt(grad_mixed, qkv_w[b])
        return grad_normed, grad_qkv, grad_proj, sums

    def collect(rows):
        return lax.psum_scatter(rows, "dp", scatter_dimension=0, tiled=True)

    def split_cols(rows, pieces):
        return rows.reshape(drow, pieces, tp, -1).transpose(2, 0, 1, 3)

    def branch_blocks(rows):
        return jnp.concatenate(
            [
                split_cols(rows[:, : 3 * width], 3).reshape(tp, drow, 3 * part),
                split_cols(rows[:, 3 * width : 4 * width], 1).reshape(tp, drow, part),
            ],
            axis=2,
        )

    fc2_rows = collect(grad_fc2)
    fc1_rows = collect(grad_fc1)
    low_s = grad_second.astype(LOW)
    grad_n2, qkv_s, proj_s, sums_s = branch_back(low_s, mixed_s, heads_s, n2, 1, space_core)
    space_rows = collect(jnp.concatenate([qkv_s, proj_s], axis=1))
    back, gain_s, shift_s = norm_back(grad_n2, first, norms[1, 0])
    grad_first = grad_second + back
    plain_first = drop_rows(grad_first).reshape(slots * tokens, width)
    low_f = to_patches(grad_first.astype(LOW)).astype(LOW)
    grad_tfc = dot_tn(summed, low_f).astype(LOW)
    low_t = dot_nt(low_f, tfc_w).astype(LOW)
    fc1_rows, fc2_rows, low_t = together(fc1_rows, fc2_rows, low_t)
    fc1_parts = line_scatter(split_cols(fc1_rows, 1).reshape(tp, drow, hidden_part))
    fc2_parts = line_scatter(split_cols(fc2_rows, 1).reshape(tp, drow, hidden_part))
    grad_n1, qkv_t, proj_t, sums_t = branch_back(low_t, mixed_t, heads_t, n1, 0, time_core)
    *fc1_parts, grad_n1 = together(*fc1_parts, grad_n1)
    *fc2_parts, grad_n1 = together(*fc2_parts, grad_n1)
    back, gain_t, shift_t = norm_back(grad_n1, inputs_t, norms[0, 0])
    sent_back = dot_tn(merge, back.astype(LOW)).astype(LOW)
    came_back = swap_blocks(cut(sent_back), -1)

    feature = jnp.stack(
        [
            gain_t,
            shift_t,
            gain_s,
            shift_s,
            gain_m,
            shift_m,
            column_sums(low_t),
            column_sums(low_f),
            column_sums(low_s),
            column_sums(grad_low),
        ]
    )
    attn_sums = jnp.stack(
        [sums_t[:width], sums_t[2 * width :], sums_s[:width], sums_s[2 * width :]]
    )
    attn_sums = (
        attn_sums.reshape(4, tp, heads_local, dp, -1).transpose(0, 3, 1, 2, 4).reshape(4, width)
    )
    hidden_sums = (
        column_sums(grad_hidden).reshape(tp, dp, tp, srow).transpose(2, 1, 0, 3).reshape(tp, width)
    )
    small_grad = jnp.concatenate([feature, attn_sums, hidden_sums]).astype(LOW)
    small_grad = jnp.pad(small_grad, ((0, 256 - small_cols), (0, 0))).T

    time_rows = collect(jnp.concatenate([qkv_t, proj_t, grad_tfc, small_grad], axis=1))
    space_rows, sent_back = together(space_rows, sent_back)
    space_done = line_total(line_scatter(branch_blocks(space_rows)))
    grad_clips = (plain_first + dot_tn(pick_plain, came_back)).reshape(slots, tokens, width)
    shared_back = time_rows[:, 4 * width :].reshape(tp, srow, shared_cols)
    time_done = line_total(
        line_scatter(
            jnp.concatenate(
                [branch_blocks(time_rows), shared_back.reshape(tp, drow, shared_cols // tp)],
                axis=2,
            )
        )
    )
    grad_qkv = jnp.stack([time_done[:, : 3 * part], space_done[:, : 3 * part]]).reshape(
        2, drow, 3, part
    )
    grad_proj = jnp.stack([time_done[:, 3 * part : 4 * part].T, space_done[:, 3 * part :].T])
    shared_done = time_done[:, 4 * part :].reshape(srow, shared_cols)
    smalls = shared_done[:, width : width + small_cols].T
    return (
        outputs,
        grad_clips,
        grad_qkv,
        grad_proj,
        line_total(fc1_parts),
        line_total(fc2_parts).T,
        smalls[10:14].reshape(attn_bias.shape),
        smalls[14 : 14 + tp].reshape(fc1_bias.shape),
        smalls[:6].reshape(3, 2, srow),
        shared_done[:, :width],
        smalls[6:10],
    )


def solution(mesh):
    return jax.shard_map(
        shards,
        mesh=mesh,
        in_specs=(
            P("dp", "tensor", None),
            P("dp"),
            P(None, "dp", None, "tensor"),
            P(None, "tensor", "dp"),
            P("dp", "tensor"),
            P("tensor", "dp"),
            P(None, None, "tensor", "dp"),
            P("tensor", "dp"),
            P(None, None, ("dp", "tensor")),
            P(("dp", "tensor"), None),
            P(None, ("dp", "tensor")),
            P("dp", "tensor", None),
        ),
        out_specs=(
            P("dp", "tensor", None),
            P("dp", "tensor", None),
            P(None, "dp", None, "tensor"),
            P(None, "tensor", "dp"),
            P("dp", "tensor"),
            P("tensor", "dp"),
            P(None, None, "tensor", "dp"),
            P("tensor", "dp"),
            P(None, None, ("dp", "tensor")),
            P(("dp", "tensor"), None),
            P(None, ("dp", "tensor")),
        ),
        check_vma=False,
    )
```

```python
from functools import partial

import jax
import jax.numpy as jnp
from jax import lax
from jax.experimental import pallas as pl
from jax.experimental.pallas import tpu as pltpu
from jax.sharding import PartitionSpec as P

FRAMES = 8
EPS = 1e-06
LOW = jnp.bfloat16
F32 = jnp.float32
NEG = -1e30


def dot_nn(left, right):
    return lax.dot_general(left, right, (((1,), (0,)), ((), ())), preferred_element_type=F32)


def dot_nt(left, right):
    return lax.dot_general(left, right, (((1,), (1,)), ((), ())), preferred_element_type=F32)


def dot_tn(left, right):
    return lax.dot_general(left, right, (((0,), (0,)), ((), ())), preferred_element_type=F32)


def line_shift(block, step):
    count = lax.axis_size("tensor")
    return lax.ppermute(block, "tensor", [(i, (i + step) % count) for i in range(count)])


def line_gather(block):
    return [block] + [line_shift(block, k) for k in range(1, lax.axis_size("tensor"))]


def line_order(back):
    count = lax.axis_size("tensor")
    place = lax.axis_index("tensor")
    return [
        lax.select_n(lax.rem(place - j + count, count), *back) for j in range(count)
    ]


def line_scatter(blocks):
    count = lax.axis_size("tensor")
    place = lax.axis_index("tensor")
    parts = []
    for k in range(count):
        ahead = lax.dynamic_index_in_dim(
            blocks, lax.rem(place + k, count), axis=0, keepdims=False
        )
        parts.append(ahead if k == 0 else line_shift(ahead, k))
    return parts


def line_total(parts):
    total = parts[0].astype(F32)
    for part in parts[1:]:
        total = total + part.astype(F32)
    return total


def swap_blocks(blocks, sign):
    count = lax.axis_size("tensor")
    moved = [blocks[0]]
    for k in range(1, count):
        pairs = [(i, (i + sign * k) % count) for i in range(count)]
        moved.append(lax.ppermute(blocks[k], "tensor", pairs))
    return jnp.concatenate(moved, axis=0)


def flip(block, mask):
    count = lax.axis_size("dp")
    return lax.ppermute(block, "dp", [(i, i ^ mask) for i in range(count)])


def is_square():
    return lax.axis_size("dp") == 8


def place_kernel(me_ref, *refs):
    pieces, out_ref = refs[:-1], refs[-1]
    for mask, piece in enumerate(pieces):
        out_ref[me_ref[0] ^ mask] = piece[...]


def place_pieces(pieces):
    shape = (len(pieces),) + pieces[0].shape
    whole = pl.BlockSpec(memory_space=pltpu.VMEM)
    out = pl.pallas_call(
        place_kernel,
        in_specs=[pl.BlockSpec(memory_space=pltpu.SMEM)] + [whole] * len(pieces),
        out_specs=whole,
        out_shape=jax.ShapeDtypeStruct(shape, pieces[0].dtype),
        compiler_params=pltpu.CompilerParams(vmem_limit_bytes=24 << 20),
        cost_estimate=pl.CostEstimate(
            flops=0, bytes_accessed=32 * pieces[0].size, transcendentals=0
        ),
        name="place_pieces",
    )(lax.axis_index("dp").astype(jnp.int32).reshape(1), *pieces)
    return out.reshape(-1, shape[2])


def chip_scatter(arrays):
    if not is_square():
        joined = jnp.concatenate(arrays, axis=1)
        return lax.psum_scatter(joined, "dp", scatter_dimension=0, tiled=True)
    me = lax.axis_index("dp")
    core, chip = me & 1, me >> 1
    height = arrays[0].shape[0] // 8

    def half(which):
        parts = [
            lax.dynamic_index_in_dim(
                item.reshape(4, 2, height, -1), which, axis=1, keepdims=False
            )
            for item in arrays
        ]
        return jnp.concatenate(parts, axis=2)

    arrived = flip(half(1 - core), 1)
    kept = (half(core).astype(F32) + arrived.astype(F32)).astype(LOW)
    total = lax.dynamic_index_in_dim(kept, chip, axis=0, keepdims=False).astype(F32)
    for mask in (1, 2, 3):
        away = lax.dynamic_index_in_dim(kept, chip ^ mask, axis=0, keepdims=False)
        total = total + flip(away, 2 * mask).astype(F32)
    return total.astype(LOW)


def pair_sides(values, first):
    wide = values.astype(F32)
    zero = jnp.zeros_like(wide)
    both = [jnp.where(first, wide, zero), jnp.where(first, zero, wide)]
    return jnp.concatenate(both, axis=0).astype(LOW)


def key_mask(rows, group, keys):
    key = lax.broadcasted_iota(jnp.int32, (2, rows, rows), 1)
    query = lax.broadcasted_iota(jnp.int32, (2, rows, rows), 2)
    if keys is not None:
        return key < keys
    return (key // group) == (query // group)


def pair_probs(query, key_sides, mask, rows):
    scores = dot_nt(key_sides, query).reshape(2, rows, rows)
    scores = jnp.where(mask, scores, NEG)
    grown = jnp.exp(scores - jnp.max(scores, axis=1, keepdims=True))
    return grown * (1.0 / jnp.sum(grown, axis=1, keepdims=True))


def attend_kernel(group, keys, width, mixed_ref, out_ref):
    rows = out_ref.shape[-2]
    mask = key_mask(rows, group, keys)
    first = lax.broadcasted_iota(jnp.int32, (rows, 128), 1) < 64
    for at in range(0, width, 128):
        query = mixed_ref[:, at : at + 128] * LOW(0.125)
        key = pair_sides(mixed_ref[:, width + at : width + at + 128], first)
        value = pair_sides(mixed_ref[:, 2 * width + at : 2 * width + at + 128], first)
        probs = pair_probs(query, key, mask, rows).reshape(2 * rows, rows)
        out_ref[:, at : at + 128] = dot_tn(probs.astype(LOW), value).astype(LOW)


def attend_back_kernel(group, keys, width, mixed_ref, grad_ref, out_ref, sums_ref):
    rows = grad_ref.shape[-2]
    mask = key_mask(rows, group, keys)
    first = lax.broadcasted_iota(jnp.int32, (rows, 128), 1) < 64

    @pl.when(pl.program_id(0) == 0)
    def clear():
        sums_ref[...] = jnp.zeros_like(sums_ref)

    for at in range(0, width, 128):
        query = mixed_ref[:, at : at + 128] * LOW(0.125)
        key = pair_sides(mixed_ref[:, width + at : width + at + 128], first)
        value = pair_sides(mixed_ref[:, 2 * width + at : 2 * width + at + 128], first)
        grad = grad_ref[:, at : at + 128]
        probs = pair_probs(query, key, mask, rows)
        grad_probs = dot_nt(value, grad).reshape(2, rows, rows)
        inner = jnp.sum(grad_probs * probs, axis=1, keepdims=True)
        grad_scores = (probs * (grad_probs - inner)).reshape(2 * rows, rows).astype(LOW)
        probs_low = probs.reshape(2 * rows, rows).astype(LOW)
        dq = (dot_tn(grad_scores, key) * 0.125).astype(LOW)
        dk = dot_nn(grad_scores, query)
        dv = dot_nn(probs_low, grad)
        dk = jnp.where(first, dk[:rows], dk[rows:]).astype(LOW)
        dv = jnp.where(first, dv[:rows], dv[rows:]).astype(LOW)
        out_ref[:, at : at + 128] = dq
        out_ref[:, width + at : width + at + 128] = dk
        out_ref[:, 2 * width + at : 2 * width + at + 128] = dv
        for part, value in ((0, dq), (2, dv)):
            start = part * width + at
            total = jnp.sum(value.astype(F32), axis=0, keepdims=True)
            sums_ref[:, start : start + 128] = sums_ref[:, start : start + 128] + total


def attend(mixed, blocks, rows, group, keys):
    width = mixed.shape[1] // 3
    out = pl.pallas_call(
        partial(attend_kernel, group, keys, width),
        grid=(blocks,),
        in_specs=[pl.BlockSpec((None, rows, 3 * width), lambda i: (i, 0, 0))],
        out_specs=pl.BlockSpec((None, rows, width), lambda i: (i, 0, 0)),
        out_shape=jax.ShapeDtypeStruct((blocks, rows, width), LOW),
        compiler_params=pltpu.CompilerParams(vmem_limit_bytes=32 << 20),
        cost_estimate=pl.CostEstimate(
            flops=8_000_000_000, bytes_accessed=8 * blocks * rows * width, transcendentals=0
        ),
        name="attend",
    )(mixed.reshape(blocks, rows, 3 * width))
    return out.reshape(blocks * rows, width)


def attend_back(mixed, grad, blocks, rows, group, keys):
    width = grad.shape[1]
    out, sums = pl.pallas_call(
        partial(attend_back_kernel, group, keys, width),
        grid=(blocks,),
        in_specs=[
            pl.BlockSpec((None, rows, 3 * width), lambda i: (i, 0, 0)),
            pl.BlockSpec((None, rows, width), lambda i: (i, 0, 0)),
        ],
        out_specs=[
            pl.BlockSpec((None, rows, 3 * width), lambda i: (i, 0, 0)),
            pl.BlockSpec((1, 3 * width), lambda i: (0, 0)),
        ],
        out_shape=[
            jax.ShapeDtypeStruct((blocks, rows, 3 * width), LOW),
            jax.ShapeDtypeStruct((1, 3 * width), F32),
        ],
        compiler_params=pltpu.CompilerParams(vmem_limit_bytes=32 << 20),
        cost_estimate=pl.CostEstimate(
            flops=18_000_000_000, bytes_accessed=14 * blocks * rows * width, transcendentals=0
        ),
        name="attend_back",
    )(mixed.reshape(blocks, rows, 3 * width), grad.reshape(blocks, rows, width))
    return out.reshape(blocks * rows, 3 * width), sums[0]


def norm_stats(rows):
    centred = rows - jnp.mean(rows, axis=-1, keepdims=True)
    scale = lax.rsqrt(jnp.mean(centred * centred, axis=-1, keepdims=True) + EPS)
    return centred * scale, scale


def norm_low(rows, gain, shift):
    return (norm_stats(rows)[0] * gain + shift).astype(LOW)


def norm_back(grad, rows, gain):
    unit, scale = norm_stats(rows)
    scaled = grad * gain
    mean_plain = jnp.mean(scaled, axis=-1, keepdims=True)
    mean_unit = jnp.mean(scaled * unit, axis=-1, keepdims=True)
    back = (scaled - mean_plain - unit * mean_unit) * scale
    return back, jnp.sum(grad * unit, axis=0), jnp.sum(grad, axis=0)


def column_sums(rows):
    return jnp.sum(rows.astype(F32), axis=0)


def together(*values):
    return lax.optimization_barrier(values)


def shards(
    clips,
    clip_live,
    qkv_weight,
    proj_weight,
    fc1_weight,
    fc2_weight,
    attn_bias,
    fc1_bias,
    norm_params,
    tfc_weight,
    out_bias,
    cotangent,
):
    tp = lax.axis_size("tensor")
    place = lax.axis_index("tensor")
    slots, tokens, width = clips.shape
    part = qkv_weight.shape[3]
    drow = qkv_weight.shape[1]
    srow = tfc_weight.shape[0]
    hidden_part = fc1_weight.shape[1]
    frames = FRAMES // tp
    patches = tokens // frames
    share = patches // tp
    padded = -(-patches // 8) * 8
    images = slots * frames
    rows_f = images * padded
    group_rows = images * share
    block_rows = -(-group_rows // 8) * 8
    rows_t = slots * share * FRAMES

    dp = width // drow
    heads_local = attn_bias.shape[2]
    small = jnp.concatenate(
        [norm_params.reshape(6, srow).T, out_bias.T, attn_bias.reshape(4, srow).T], axis=1
    )
    shared_cols = width + 256
    shared = jnp.concatenate(
        [
            tfc_weight,
            jnp.pad(small, ((0, 0), (0, 128 - small.shape[1]))),
            jnp.pad(fc1_bias, ((0, srow - 1), (0, 128 - drow))),
        ],
        axis=1,
    ).reshape(drow, shared_cols // tp)

    def branch_rows(pieces):
        parts = [
            piece[:, k * part : (k + 1) * part] for k in range(4) for piece in line_order(pieces)
        ]
        return jnp.concatenate(parts, axis=1)

    dims = (dp, tp, heads_local, srow // heads_local, width)
    at_dp, at_place, at_head, at_lane = (
        lax.broadcasted_iota(jnp.int32, dims, d) for d in range(4)
    )
    column = lax.broadcasted_iota(jnp.int32, dims, 4)
    lanes = srow // heads_local
    head_order = ((at_place * heads_local + at_head) * dp + at_dp) * lanes + at_lane == column
    row = lax.broadcasted_iota(jnp.int32, (width, width), 0)
    column = lax.broadcasted_iota(jnp.int32, (width, width), 1)
    orders = jnp.concatenate([row == column, head_order.reshape(width, width)], axis=1)
    orders = orders.astype(LOW)

    def spread(rows):
        return lax.all_gather(rows, "dp", axis=0, tiled=True)

    def cut(rows):
        return [rows[k * block_rows : (k + 1) * block_rows] for k in range(tp)]

    def pick_rows(columns):
        dims = (tp, block_rows, images, columns)
        shift, row, image, patch = (lax.broadcasted_iota(jnp.int32, dims, d) for d in range(4))
        target = lax.rem(place + shift, tp)
        found = ((row // share) == image) & ((row % share) + target * share == patch)
        return (found & (row < group_rows)).astype(LOW).reshape(tp * block_rows, images * columns)

    pick = pick_rows(padded)
    pick_plain = pick_rows(patches)
    dims = (rows_t, tp, block_rows)
    row, shift, sent = (lax.broadcasted_iota(jnp.int32, dims, d) for d in range(3))
    frame = row % FRAMES
    merge = ((frame // frames) == lax.rem(place - shift + tp, tp)) & (
        ((row // (FRAMES * share)) * frames + frame % frames) * share + (row // FRAMES) % share
        == sent
    )
    merge = merge.astype(LOW).reshape(rows_t, tp * block_rows)

    time_own = jnp.concatenate(
        [qkv_weight[0].reshape(drow, 3 * part), proj_weight[0].T, shared], axis=1
    )
    space_own = jnp.concatenate([qkv_weight[1].reshape(drow, 3 * part), proj_weight[1].T], axis=1)
    fc2_own = fc2_weight.T
    sent_x = dot_nn(pick_plain, clips.reshape(slots * tokens, width)).astype(LOW)
    time_back = line_gather(time_own)
    *time_back, held_x = together(*time_back, sent_x)
    came_x = swap_blocks(cut(held_x)[:1] + cut(sent_x)[1:], 1)
    space_own, held_x = together(space_own, sent_x)
    space_back = line_gather(space_own)
    shared_rows = jnp.concatenate(
        [piece[:, 4 * part :].reshape(srow, shared_cols) for piece in line_order(time_back)]
    )
    time_all = spread(jnp.concatenate([branch_rows(time_back), shared_rows], axis=1))
    fc1_own, came_x = together(fc1_weight, came_x)
    fc1_back = line_gather(fc1_own)
    fc2_own, time_all = together(fc2_own, time_all)
    fc2_back = line_gather(fc2_own)
    space_all = spread(branch_rows(space_back))
    fc1_w = spread(jnp.concatenate(line_order(fc1_back), axis=1))
    qkv_w = (time_all[:, : 3 * width], space_all[:, : 3 * width])
    proj_w = (time_all[:, 3 * width : 4 * width], space_all[:, 3 * width :])
    tfc_w = time_all[:, 4 * width : 5 * width]
    small_all = dot_tn(time_all[:, 5 * width : 5 * width + 16], orders)
    norms = small_all[:6, :width].reshape(3, 2, width)
    out_b = small_all[6:10, :width]
    attn_b = small_all[10:14, width:].reshape(2, 2, width)
    hidden_b = time_all[:, 5 * width + 128 : 5 * width + 128 + drow].reshape(dp, tp, srow, drow)
    hidden_b = hidden_b[:, :, 0].transpose(1, 0, 2).reshape(-1).astype(F32)
    bias_rows = [
        jnp.concatenate([attn_b[b, 0], jnp.zeros((width,), F32), attn_b[b, 1]]) for b in (0, 1)
    ]

    def to_patches(rows):
        sent = dot_nn(pick, rows).astype(LOW)
        return dot_nn(merge, swap_blocks(cut(sent), 1))

    def pad_rows(values):
        shaped = values.reshape(images, patches, width)
        return jnp.pad(shaped, ((0, 0), (0, padded - patches), (0, 0))).reshape(rows_f, width)

    def drop_rows(values):
        return values.reshape(images, padded, width)[:, :patches].reshape(slots, tokens, width)

    inputs_low = pad_rows(clips)
    live = jnp.repeat(clip_live.astype(F32), frames * padded)[:, None]

    def qkv_of(normed, b):
        return (dot_nn(normed, qkv_w[b]) + bias_rows[b]).astype(LOW)

    time_blocks = 1
    while rows_t // time_blocks > 128 or rows_t % (8 * time_blocks):
        time_blocks += 1
    time_core = (time_blocks, rows_t // time_blocks, FRAMES, None)
    space_core = (images, padded, None, patches)

    inputs_t = dot_nn(merge, came_x)
    n1 = norm_low(inputs_t, norms[0, 0], norms[0, 1])
    mixed_t = qkv_of(n1, 0)
    heads_t = attend(mixed_t, *time_core)
    *fc2_back, heads_t = together(*fc2_back, heads_t)
    summed = (dot_nt(heads_t, proj_w[0]) + out_b[0]).astype(LOW)
    moved = (dot_nn(summed, tfc_w) + out_b[1]).astype(LOW)
    came_f = swap_blocks(cut(dot_tn(merge, moved).astype(LOW)), -1)
    first = inputs_low.astype(F32) + dot_tn(pick, came_f)
    n2 = norm_low(first, norms[1, 0], norms[1, 1])
    mixed_s = qkv_of(n2, 1)
    *fc2_back, mixed_s = together(*fc2_back, mixed_s)
    fc2_rows = jnp.concatenate(line_order(fc2_back), axis=1)
    if is_square():
        fc2_chips = [fc2_rows] + [flip(fc2_rows, mask) for mask in (2, 4, 6)]
    heads_s = attend(mixed_s, *space_core)
    second = first + dot_nt(heads_s, proj_w[1]) + out_b[2]
    n3 = norm_low(second, norms[2, 0], norms[2, 1])
    hidden = dot_nn(n3, fc1_w) + hidden_b
    cdf = 0.5 * (1.0 + lax.erf(hidden * (2.0**-0.5)))
    active = (hidden * cdf).astype(LOW)
    slope = (cdf + hidden * jnp.exp(-0.5 * hidden * hidden) * 0.3989422804014327).astype(LOW)
    if is_square():
        *fc2_chips, active = together(*fc2_chips, active)
        fc2_pairs = [flip(piece, 1) for piece in fc2_chips]
        fc2_w = place_pieces([piece for pair in zip(fc2_chips, fc2_pairs) for piece in pair])
    else:
        fc2_w = spread(fc2_rows)

    grad_result = pad_rows(cotangent).astype(F32) * live
    grad_low = grad_result.astype(LOW)
    grad_fc2 = dot_tn(grad_low, active).astype(LOW)
    grad_fc2, grad_low = together(grad_fc2, grad_low)
    grad_hidden = (dot_nn(grad_low, fc2_w) * slope.astype(F32)).astype(LOW)
    grad_fc1 = dot_tn(n3, grad_hidden).astype(LOW)
    grad_fc1, grad_hidden = together(grad_fc1, grad_hidden)
    grad_n3 = dot_nt(grad_hidden, fc1_w)
    back, gain_m, shift_m = norm_back(grad_n3, second, norms[2, 0])
    grad_second = grad_result + back

    def branch_back(low, mixed, normed, b, core, held):
        grad_heads = dot_nn(low, proj_w[b]).astype(LOW)
        grad_mixed, sums = attend_back(mixed, grad_heads, *core)
        held, grad_mixed = together(held, grad_mixed)
        parts = line_scatter(blocks_of(held, 1))
        grad_qkv = dot_tn(normed, grad_mixed).astype(LOW)
        grad_normed = dot_nt(grad_mixed, qkv_w[b])
        return grad_normed, grad_qkv, sums, parts

    def collect(rows):
        return lax.psum_scatter(rows, "dp", scatter_dimension=0, tiled=True)

    def split_cols(rows, pieces):
        return rows.reshape(drow, pieces, tp, -1).transpose(2, 0, 1, 3)

    def blocks_of(rows, pieces):
        return split_cols(rows, pieces).reshape(tp, drow, rows.shape[1] // tp)

    fc2_rows = collect(grad_fc2)
    fc1_rows = collect(grad_fc1)
    low_s = grad_second.astype(LOW)
    proj_s = dot_tn(low_s, heads_s).astype(LOW)
    grad_n2, qkv_s, sums_s, fc2_parts = branch_back(low_s, mixed_s, n2, 1, space_core, fc2_rows)
    back, gain_s, shift_s = norm_back(grad_n2, first, norms[1, 0])
    grad_first = grad_second + back
    plain_first = drop_rows(grad_first).reshape(slots * tokens, width)
    low_f = to_patches(grad_first.astype(LOW)).astype(LOW)
    grad_tfc = dot_tn(summed, low_f).astype(LOW)
    low_t = dot_nt(low_f, tfc_w).astype(LOW)
    proj_t = dot_tn(low_t, heads_t).astype(LOW)
    middle_rows = jnp.concatenate([qkv_s, proj_s, proj_t, grad_tfc], axis=1)
    middle_rows, low_t = together(middle_rows, low_t)
    middle_rows = collect(middle_rows)
    grad_n1, qkv_t, sums_t, fc1_parts = branch_back(low_t, mixed_t, n1, 0, time_core, fc1_rows)
    active, grad_n1 = together(active, grad_n1)
    result = second + dot_nt(active, fc2_w) + out_b[3]
    outputs = drop_rows((result * live).astype(LOW))
    back, gain_t, shift_t = norm_back(grad_n1, inputs_t, norms[0, 0])
    sent_back = dot_tn(merge, back.astype(LOW)).astype(LOW)
    came_back = swap_blocks(cut(sent_back), -1)

    feature = jnp.stack(
        [
            gain_t,
            shift_t,
            gain_s,
            shift_s,
            gain_m,
            shift_m,
            column_sums(low_t),
            column_sums(low_f),
            column_sums(low_s),
            column_sums(grad_low),
        ]
    )
    attn_sums = jnp.stack(
        [sums_t[:width], sums_t[2 * width :], sums_s[:width], sums_s[2 * width :]]
    )
    rows = jnp.concatenate(
        [
            jnp.pad(feature, ((0, 0), (0, width))),
            jnp.pad(attn_sums, ((0, 128 - 14), (width, 0))),
        ]
    ).astype(LOW)
    hidden_sums = column_sums(grad_hidden).reshape(tp, dp, 1, drow).transpose(1, 0, 2, 3)
    hidden_sums = jnp.pad(hidden_sums, ((0, 0), (0, 0), (0, srow - 1), (0, 128 - drow)))
    last_rows = chip_scatter(
        [qkv_t, dot_nt(orders, rows).astype(LOW), hidden_sums.reshape(width, 128).astype(LOW)]
    )
    last_rows, came_back = together(last_rows, came_back)
    middle = jnp.concatenate(
        [
            blocks_of(middle_rows[:, : 3 * width], 3),
            blocks_of(middle_rows[:, 3 * width : 4 * width], 1),
            blocks_of(middle_rows[:, 4 * width : 5 * width], 1),
            middle_rows[:, 5 * width :].reshape(tp, drow, part),
        ],
        axis=2,
    )
    middle = line_total(line_scatter(middle))
    last = jnp.concatenate(
        [
            blocks_of(last_rows[:, : 3 * width], 3),
            last_rows[:, 3 * width :].reshape(tp, drow, 256 // tp),
        ],
        axis=2,
    )
    last = line_total(line_scatter(last))
    grad_clips = (plain_first + dot_tn(pick_plain, came_back)).reshape(slots, tokens, width)
    grad_qkv = jnp.stack([last[:, : 3 * part], middle[:, : 3 * part]]).reshape(2, drow, 3, part)
    grad_proj = jnp.stack([middle[:, 4 * part : 5 * part].T, middle[:, 3 * part : 4 * part].T])
    grad_tfc = middle[:, 5 * part :].reshape(srow, width)
    smalls = last[:, 3 * part :].reshape(srow, 256)
    features = smalls[:, :14].T
    return (
        outputs,
        grad_clips,
        grad_qkv,
        grad_proj,
        line_total(fc1_parts),
        line_total(fc2_parts).T,
        features[10:14].reshape(attn_bias.shape),
        smalls[:1, 128 : 128 + drow],
        features[:6].reshape(3, 2, srow),
        grad_tfc,
        features[6:10],
    )


def solution(mesh):
    return jax.shard_map(
        shards,
        mesh=mesh,
        in_specs=(
            P("dp", "tensor", None),
            P("dp"),
            P(None, "dp", None, "tensor"),
            P(None, "tensor", "dp"),
            P("dp", "tensor"),
            P("tensor", "dp"),
            P(None, None, "tensor", "dp"),
            P("tensor", "dp"),
            P(None, None, ("dp", "tensor")),
            P(("dp", "tensor"), None),
            P(None, ("dp", "tensor")),
            P("dp", "tensor", None),
        ),
        out_specs=(
            P("dp", "tensor", None),
            P("dp", "tensor", None),
            P(None, "dp", None, "tensor"),
            P(None, "tensor", "dp"),
            P("dp", "tensor"),
            P("tensor", "dp"),
            P(None, None, "tensor", "dp"),
            P("tensor", "dp"),
            P(None, None, ("dp", "tensor")),
            P(("dp", "tensor"), None),
            P(None, ("dp", "tensor")),
        ),
        check_vma=False,
    )
```

```python
from functools import partial

import jax
import jax.numpy as jnp
from jax import lax
from jax.experimental import pallas as pl
from jax.experimental.pallas import tpu as pltpu
from jax.sharding import PartitionSpec as P

FRAMES = 8
EPS = 1e-06
LOW = jnp.bfloat16
F32 = jnp.float32
NEG = -1e30


def dot_nn(left, right):
    return lax.dot_general(left, right, (((1,), (0,)), ((), ())), preferred_element_type=F32)


def dot_nt(left, right):
    return lax.dot_general(left, right, (((1,), (1,)), ((), ())), preferred_element_type=F32)


def dot_tn(left, right):
    return lax.dot_general(left, right, (((0,), (0,)), ((), ())), preferred_element_type=F32)


def line_shift(block, step):
    count = lax.axis_size("tensor")
    return lax.ppermute(block, "tensor", [(i, (i + step) % count) for i in range(count)])


def line_gather(block):
    return [block] + [line_shift(block, k) for k in range(1, lax.axis_size("tensor"))]


def line_order(back):
    count = lax.axis_size("tensor")
    place = lax.axis_index("tensor")
    return [
        lax.select_n(lax.rem(place - j + count, count), *back) for j in range(count)
    ]


def line_scatter(blocks):
    count = lax.axis_size("tensor")
    place = lax.axis_index("tensor")
    parts = []
    for k in range(count):
        ahead = lax.dynamic_index_in_dim(
            blocks, lax.rem(place + k, count), axis=0, keepdims=False
        )
        parts.append(ahead if k == 0 else line_shift(ahead, k))
    return parts


def line_total(parts):
    total = parts[0].astype(F32)
    for part in parts[1:]:
        total = total + part.astype(F32)
    return total


def swap_blocks(blocks, sign):
    count = lax.axis_size("tensor")
    moved = [blocks[0]]
    for k in range(1, count):
        pairs = [(i, (i + sign * k) % count) for i in range(count)]
        moved.append(lax.ppermute(blocks[k], "tensor", pairs))
    return jnp.concatenate(moved, axis=0)


def flip(block, mask):
    count = lax.axis_size("dp")
    return lax.ppermute(block, "dp", [(i, i ^ mask) for i in range(count)])


def is_square():
    return lax.axis_size("dp") == 8


def place_kernel(me_ref, *refs):
    pieces, out_ref = refs[:-1], refs[-1]
    for mask, piece in enumerate(pieces):
        out_ref[me_ref[0] ^ mask] = piece[...]


def place_pieces(pieces):
    shape = (len(pieces),) + pieces[0].shape
    whole = pl.BlockSpec(memory_space=pltpu.VMEM)
    out = pl.pallas_call(
        place_kernel,
        in_specs=[pl.BlockSpec(memory_space=pltpu.SMEM)] + [whole] * len(pieces),
        out_specs=whole,
        out_shape=jax.ShapeDtypeStruct(shape, pieces[0].dtype),
        compiler_params=pltpu.CompilerParams(vmem_limit_bytes=24 << 20),
        cost_estimate=pl.CostEstimate(
            flops=0, bytes_accessed=32 * pieces[0].size, transcendentals=0
        ),
        name="place_pieces",
    )(lax.axis_index("dp").astype(jnp.int32).reshape(1), *pieces)
    return out.reshape(-1, shape[2])


def chip_scatter(arrays):
    if not is_square():
        joined = jnp.concatenate(arrays, axis=1)
        return lax.psum_scatter(joined, "dp", scatter_dimension=0, tiled=True)
    me = lax.axis_index("dp")
    core, chip = me & 1, me >> 1
    height = arrays[0].shape[0] // 8

    def half(which):
        parts = [
            lax.dynamic_index_in_dim(
                item.reshape(4, 2, height, -1), which, axis=1, keepdims=False
            )
            for item in arrays
        ]
        return jnp.concatenate(parts, axis=2)

    arrived = flip(half(1 - core), 1)
    kept = (half(core).astype(F32) + arrived.astype(F32)).astype(LOW)
    total = lax.dynamic_index_in_dim(kept, chip, axis=0, keepdims=False).astype(F32)
    for mask in (1, 2, 3):
        away = lax.dynamic_index_in_dim(kept, chip ^ mask, axis=0, keepdims=False)
        total = total + flip(away, 2 * mask).astype(F32)
    return total.astype(LOW)


def pair_sides(values, first):
    wide = values.astype(F32)
    zero = jnp.zeros_like(wide)
    both = [jnp.where(first, wide, zero), jnp.where(first, zero, wide)]
    return jnp.concatenate(both, axis=0).astype(LOW)


def key_mask(rows, group, keys):
    key = lax.broadcasted_iota(jnp.int32, (2, rows, rows), 1)
    query = lax.broadcasted_iota(jnp.int32, (2, rows, rows), 2)
    if keys is not None:
        return key < keys
    return (key // group) == (query // group)


def pair_probs(query, key_sides, mask, rows):
    scores = dot_nt(key_sides, query).reshape(2, rows, rows)
    scores = jnp.where(mask, scores, NEG)
    grown = jnp.exp(scores - jnp.max(scores, axis=1, keepdims=True))
    return grown * (1.0 / jnp.sum(grown, axis=1, keepdims=True))


def attend_kernel(group, keys, width, mixed_ref, out_ref):
    rows = out_ref.shape[-2]
    mask = key_mask(rows, group, keys)
    first = lax.broadcasted_iota(jnp.int32, (rows, 128), 1) < 64
    for at in range(0, width, 128):
        query = mixed_ref[:, at : at + 128] * LOW(0.125)
        key = pair_sides(mixed_ref[:, width + at : width + at + 128], first)
        value = pair_sides(mixed_ref[:, 2 * width + at : 2 * width + at + 128], first)
        probs = pair_probs(query, key, mask, rows).reshape(2 * rows, rows)
        out_ref[:, at : at + 128] = dot_tn(probs.astype(LOW), value).astype(LOW)


def attend_back_kernel(group, keys, width, mixed_ref, grad_ref, out_ref, sums_ref):
    rows = grad_ref.shape[-2]
    mask = key_mask(rows, group, keys)
    first = lax.broadcasted_iota(jnp.int32, (rows, 128), 1) < 64

    @pl.when(pl.program_id(0) == 0)
    def clear():
        sums_ref[...] = jnp.zeros_like(sums_ref)

    for at in range(0, width, 128):
        query = mixed_ref[:, at : at + 128] * LOW(0.125)
        key = pair_sides(mixed_ref[:, width + at : width + at + 128], first)
        value = pair_sides(mixed_ref[:, 2 * width + at : 2 * width + at + 128], first)
        grad = grad_ref[:, at : at + 128]
        probs = pair_probs(query, key, mask, rows)
        grad_probs = dot_nt(value, grad).reshape(2, rows, rows)
        inner = jnp.sum(grad_probs * probs, axis=1, keepdims=True)
        grad_scores = (probs * (grad_probs - inner)).reshape(2 * rows, rows).astype(LOW)
        probs_low = probs.reshape(2 * rows, rows).astype(LOW)
        dq = (dot_tn(grad_scores, key) * 0.125).astype(LOW)
        dk = dot_nn(grad_scores, query)
        dv = dot_nn(probs_low, grad)
        dk = jnp.where(first, dk[:rows], dk[rows:]).astype(LOW)
        dv = jnp.where(first, dv[:rows], dv[rows:]).astype(LOW)
        out_ref[:, at : at + 128] = dq
        out_ref[:, width + at : width + at + 128] = dk
        out_ref[:, 2 * width + at : 2 * width + at + 128] = dv
        for part, value in ((0, dq), (2, dv)):
            start = part * width + at
            total = jnp.sum(value.astype(F32), axis=0, keepdims=True)
            sums_ref[:, start : start + 128] = sums_ref[:, start : start + 128] + total


def attend(mixed, blocks, rows, group, keys):
    width = mixed.shape[1] // 3
    out = pl.pallas_call(
        partial(attend_kernel, group, keys, width),
        grid=(blocks,),
        in_specs=[pl.BlockSpec((None, rows, 3 * width), lambda i: (i, 0, 0))],
        out_specs=pl.BlockSpec((None, rows, width), lambda i: (i, 0, 0)),
        out_shape=jax.ShapeDtypeStruct((blocks, rows, width), LOW),
        compiler_params=pltpu.CompilerParams(vmem_limit_bytes=32 << 20),
        cost_estimate=pl.CostEstimate(
            flops=8_000_000_000, bytes_accessed=8 * blocks * rows * width, transcendentals=0
        ),
        name="attend",
    )(mixed.reshape(blocks, rows, 3 * width))
    return out.reshape(blocks * rows, width)


def attend_back(mixed, grad, blocks, rows, group, keys):
    width = grad.shape[1]
    out, sums = pl.pallas_call(
        partial(attend_back_kernel, group, keys, width),
        grid=(blocks,),
        in_specs=[
            pl.BlockSpec((None, rows, 3 * width), lambda i: (i, 0, 0)),
            pl.BlockSpec((None, rows, width), lambda i: (i, 0, 0)),
        ],
        out_specs=[
            pl.BlockSpec((None, rows, 3 * width), lambda i: (i, 0, 0)),
            pl.BlockSpec((1, 3 * width), lambda i: (0, 0)),
        ],
        out_shape=[
            jax.ShapeDtypeStruct((blocks, rows, 3 * width), LOW),
            jax.ShapeDtypeStruct((1, 3 * width), F32),
        ],
        compiler_params=pltpu.CompilerParams(vmem_limit_bytes=32 << 20),
        cost_estimate=pl.CostEstimate(
            flops=18_000_000_000, bytes_accessed=14 * blocks * rows * width, transcendentals=0
        ),
        name="attend_back",
    )(mixed.reshape(blocks, rows, 3 * width), grad.reshape(blocks, rows, width))
    return out.reshape(blocks * rows, 3 * width), sums[0]


def norm_stats(rows):
    centred = rows - jnp.mean(rows, axis=-1, keepdims=True)
    scale = lax.rsqrt(jnp.mean(centred * centred, axis=-1, keepdims=True) + EPS)
    return centred * scale, scale


def norm_low(rows, gain, shift):
    return (norm_stats(rows)[0] * gain + shift).astype(LOW)


def norm_back(grad, rows, gain):
    unit, scale = norm_stats(rows)
    scaled = grad * gain
    mean_plain = jnp.mean(scaled, axis=-1, keepdims=True)
    mean_unit = jnp.mean(scaled * unit, axis=-1, keepdims=True)
    back = (scaled - mean_plain - unit * mean_unit) * scale
    return back, jnp.sum(grad * unit, axis=0), jnp.sum(grad, axis=0)


def column_sums(rows):
    return jnp.sum(rows.astype(F32), axis=0)


def together(*values):
    return lax.optimization_barrier(values)


def shards(
    clips,
    clip_live,
    qkv_weight,
    proj_weight,
    fc1_weight,
    fc2_weight,
    attn_bias,
    fc1_bias,
    norm_params,
    tfc_weight,
    out_bias,
    cotangent,
):
    tp = lax.axis_size("tensor")
    place = lax.axis_index("tensor")
    slots, tokens, width = clips.shape
    part = qkv_weight.shape[3]
    drow = qkv_weight.shape[1]
    srow = tfc_weight.shape[0]
    hidden_part = fc1_weight.shape[1]
    frames = FRAMES // tp
    patches = tokens // frames
    share = patches // tp
    padded = -(-patches // 8) * 8
    images = slots * frames
    rows_f = images * padded
    group_rows = images * share
    block_rows = -(-group_rows // 8) * 8
    rows_t = slots * share * FRAMES

    dp = width // drow
    heads_local = attn_bias.shape[2]
    small = jnp.concatenate(
        [norm_params.reshape(6, srow).T, out_bias.T, attn_bias.reshape(4, srow).T], axis=1
    )
    shared_cols = width + 256
    shared = jnp.concatenate(
        [
            tfc_weight,
            jnp.pad(small, ((0, 0), (0, 128 - small.shape[1]))),
            jnp.pad(fc1_bias, ((0, srow - 1), (0, 128 - drow))),
        ],
        axis=1,
    ).reshape(drow, shared_cols // tp)

    def branch_rows(pieces):
        parts = [
            piece[:, k * part : (k + 1) * part] for k in range(4) for piece in line_order(pieces)
        ]
        return jnp.concatenate(parts, axis=1)

    dims = (dp, tp, heads_local, srow // heads_local, width)
    at_dp, at_place, at_head, at_lane = (
        lax.broadcasted_iota(jnp.int32, dims, d) for d in range(4)
    )
    column = lax.broadcasted_iota(jnp.int32, dims, 4)
    lanes = srow // heads_local
    head_order = ((at_place * heads_local + at_head) * dp + at_dp) * lanes + at_lane == column
    row = lax.broadcasted_iota(jnp.int32, (width, width), 0)
    column = lax.broadcasted_iota(jnp.int32, (width, width), 1)
    orders = jnp.concatenate([row == column, head_order.reshape(width, width)], axis=1)
    orders = orders.astype(LOW)

    def spread(rows):
        return lax.all_gather(rows, "dp", axis=0, tiled=True)

    def cut(rows):
        return [rows[k * block_rows : (k + 1) * block_rows] for k in range(tp)]

    def pick_rows(columns):
        dims = (tp, block_rows, images, columns)
        shift, row, image, patch = (lax.broadcasted_iota(jnp.int32, dims, d) for d in range(4))
        target = lax.rem(place + shift, tp)
        found = ((row // share) == image) & ((row % share) + target * share == patch)
        return (found & (row < group_rows)).astype(LOW).reshape(tp * block_rows, images * columns)

    pick = pick_rows(padded)
    pick_plain = pick_rows(patches)
    dims = (rows_t, tp, block_rows)
    row, shift, sent = (lax.broadcasted_iota(jnp.int32, dims, d) for d in range(3))
    frame = row % FRAMES
    merge = ((frame // frames) == lax.rem(place - shift + tp, tp)) & (
        ((row // (FRAMES * share)) * frames + frame % frames) * share + (row // FRAMES) % share
        == sent
    )
    merge = merge.astype(LOW).reshape(rows_t, tp * block_rows)

    time_own = jnp.concatenate(
        [qkv_weight[0].reshape(drow, 3 * part), proj_weight[0].T, shared], axis=1
    )
    space_own = jnp.concatenate([qkv_weight[1].reshape(drow, 3 * part), proj_weight[1].T], axis=1)
    fc2_own = fc2_weight.T
    sent_x = dot_nn(pick_plain, clips.reshape(slots * tokens, width)).astype(LOW)
    time_back = line_gather(time_own)
    *time_back, held_x = together(*time_back, sent_x)
    came_x = swap_blocks(cut(held_x)[:1] + cut(sent_x)[1:], 1)
    space_own, held_x = together(space_own, sent_x)
    space_back = line_gather(space_own)
    shared_rows = jnp.concatenate(
        [piece[:, 4 * part :].reshape(srow, shared_cols) for piece in line_order(time_back)]
    )
    time_all = spread(jnp.concatenate([branch_rows(time_back), shared_rows], axis=1))
    fc1_own, held_x = together(fc1_weight, sent_x)
    fc1_back = line_gather(fc1_own)
    *fc1_back, came_x = together(*fc1_back, came_x)
    fc2_own, time_all = together(fc2_own, time_all)
    fc2_back = line_gather(fc2_own)
    space_all = spread(branch_rows(space_back))
    fc1_w = spread(jnp.concatenate(line_order(fc1_back), axis=1))
    qkv_w = (time_all[:, : 3 * width], space_all[:, : 3 * width])
    proj_w = (time_all[:, 3 * width : 4 * width], space_all[:, 3 * width :])
    tfc_w = time_all[:, 4 * width : 5 * width]
    small_all = dot_tn(time_all[:, 5 * width : 5 * width + 16], orders)
    norms = small_all[:6, :width].reshape(3, 2, width)
    out_b = small_all[6:10, :width]
    attn_b = small_all[10:14, width:].reshape(2, 2, width)
    hidden_b = time_all[:, 5 * width + 128 : 5 * width + 128 + drow].reshape(dp, tp, srow, drow)
    hidden_b = hidden_b[:, :, 0].transpose(1, 0, 2).reshape(-1).astype(F32)
    bias_rows = [
        jnp.concatenate([attn_b[b, 0], jnp.zeros((width,), F32), attn_b[b, 1]]) for b in (0, 1)
    ]

    def to_patches(rows):
        sent = dot_nn(pick, rows).astype(LOW)
        return dot_nn(merge, swap_blocks(cut(sent), 1))

    def pad_rows(values):
        shaped = values.reshape(images, patches, width)
        return jnp.pad(shaped, ((0, 0), (0, padded - patches), (0, 0))).reshape(rows_f, width)

    def drop_rows(values):
        return values.reshape(images, padded, width)[:, :patches].reshape(slots, tokens, width)

    inputs_low = pad_rows(clips)
    live = jnp.repeat(clip_live.astype(F32), frames * padded)[:, None]

    def qkv_of(normed, b):
        return (dot_nn(normed, qkv_w[b]) + bias_rows[b]).astype(LOW)

    time_blocks = 1
    while rows_t // time_blocks > 128 or rows_t % (8 * time_blocks):
        time_blocks += 1
    time_core = (time_blocks, rows_t // time_blocks, FRAMES, None)
    space_core = (images, padded, None, patches)

    inputs_t = dot_nn(merge, came_x)
    n1 = norm_low(inputs_t, norms[0, 0], norms[0, 1])
    mixed_t = qkv_of(n1, 0)
    heads_t = attend(mixed_t, *time_core)
    *fc2_back, heads_t = together(*fc2_back, heads_t)
    summed = (dot_nt(heads_t, proj_w[0]) + out_b[0]).astype(LOW)
    moved = (dot_nn(summed, tfc_w) + out_b[1]).astype(LOW)
    came_f = swap_blocks(cut(dot_tn(merge, moved).astype(LOW)), -1)
    first = inputs_low.astype(F32) + dot_tn(pick, came_f)
    n2 = norm_low(first, norms[1, 0], norms[1, 1])
    mixed_s = qkv_of(n2, 1)
    *fc2_back, mixed_s = together(*fc2_back, mixed_s)
    fc2_rows = jnp.concatenate(line_order(fc2_back), axis=1)
    if is_square():
        fc2_chips = [fc2_rows] + [flip(fc2_rows, mask) for mask in (2, 4, 6)]
    heads_s = attend(mixed_s, *space_core)
    second = first + dot_nt(heads_s, proj_w[1]) + out_b[2]
    n3 = norm_low(second, norms[2, 0], norms[2, 1])
    hidden = dot_nn(n3, fc1_w) + hidden_b
    cdf = 0.5 * (1.0 + lax.erf(hidden * (2.0**-0.5)))
    active = (hidden * cdf).astype(LOW)
    slope = (cdf + hidden * jnp.exp(-0.5 * hidden * hidden) * 0.3989422804014327).astype(LOW)
    if is_square():
        *fc2_chips, active = together(*fc2_chips, active)
        fc2_pairs = [flip(piece, 1) for piece in fc2_chips]
        fc2_w = place_pieces([piece for pair in zip(fc2_chips, fc2_pairs) for piece in pair])
    else:
        fc2_w = spread(fc2_rows)

    grad_result = pad_rows(cotangent).astype(F32) * live
    grad_low = grad_result.astype(LOW)
    grad_fc2 = dot_tn(grad_low, active).astype(LOW)
    grad_fc2, grad_low = together(grad_fc2, grad_low)
    grad_hidden = (dot_nn(grad_low, fc2_w) * slope.astype(F32)).astype(LOW)
    grad_fc1 = dot_tn(n3, grad_hidden).astype(LOW)
    grad_fc1, grad_hidden = together(grad_fc1, grad_hidden)
    grad_n3 = dot_nt(grad_hidden, fc1_w)
    back, gain_m, shift_m = norm_back(grad_n3, second, norms[2, 0])
    grad_second = grad_result + back

    def branch_back(low, mixed, normed, b, core, held):
        grad_heads = dot_nn(low, proj_w[b]).astype(LOW)
        grad_mixed, sums = attend_back(mixed, grad_heads, *core)
        held, grad_mixed = together(held, grad_mixed)
        parts = line_scatter(blocks_of(held, 1))
        grad_qkv = dot_tn(normed, grad_mixed).astype(LOW)
        grad_normed = dot_nt(grad_mixed, qkv_w[b])
        return grad_normed, grad_qkv, sums, parts

    def collect(rows):
        return lax.psum_scatter(rows, "dp", scatter_dimension=0, tiled=True)

    def split_cols(rows, pieces):
        return rows.reshape(drow, pieces, tp, -1).transpose(2, 0, 1, 3)

    def blocks_of(rows, pieces):
        return split_cols(rows, pieces).reshape(tp, drow, rows.shape[1] // tp)

    fc2_rows = collect(grad_fc2)
    fc1_rows = collect(grad_fc1)
    low_s = grad_second.astype(LOW)
    proj_s = dot_tn(low_s, heads_s).astype(LOW)
    grad_n2, qkv_s, sums_s, fc2_parts = branch_back(low_s, mixed_s, n2, 1, space_core, fc2_rows)
    back, gain_s, shift_s = norm_back(grad_n2, first, norms[1, 0])
    grad_first = grad_second + back
    plain_first = drop_rows(grad_first).reshape(slots * tokens, width)
    low_f = to_patches(grad_first.astype(LOW)).astype(LOW)
    grad_tfc = dot_tn(summed, low_f).astype(LOW)
    low_t = dot_nt(low_f, tfc_w).astype(LOW)
    proj_t = dot_tn(low_t, heads_t).astype(LOW)
    middle_rows = jnp.concatenate([qkv_s, proj_s, proj_t, grad_tfc], axis=1)
    middle_rows, low_t = together(middle_rows, low_t)
    middle_rows = collect(middle_rows)
    grad_n1, qkv_t, sums_t, fc1_parts = branch_back(low_t, mixed_t, n1, 0, time_core, fc1_rows)
    active, grad_n1 = together(active, grad_n1)
    result = second + dot_nt(active, fc2_w) + out_b[3]
    outputs = drop_rows((result * live).astype(LOW))
    back, gain_t, shift_t = norm_back(grad_n1, inputs_t, norms[0, 0])
    sent_back = dot_tn(merge, back.astype(LOW)).astype(LOW)
    came_back = swap_blocks(cut(sent_back), -1)

    feature = jnp.stack(
        [
            gain_t,
            shift_t,
            gain_s,
            shift_s,
            gain_m,
            shift_m,
            column_sums(low_t),
            column_sums(low_f),
            column_sums(low_s),
            column_sums(grad_low),
        ]
    )
    attn_sums = jnp.stack(
        [sums_t[:width], sums_t[2 * width :], sums_s[:width], sums_s[2 * width :]]
    )
    rows = jnp.concatenate(
        [
            jnp.pad(feature, ((0, 0), (0, width))),
            jnp.pad(attn_sums, ((0, 128 - 14), (width, 0))),
        ]
    ).astype(LOW)
    hidden_sums = column_sums(grad_hidden).reshape(tp, dp, 1, drow).transpose(1, 0, 2, 3)
    hidden_sums = jnp.pad(hidden_sums, ((0, 0), (0, 0), (0, srow - 1), (0, 128 - drow)))
    last_rows = chip_scatter(
        [qkv_t, dot_nt(orders, rows).astype(LOW), hidden_sums.reshape(width, 128).astype(LOW)]
    )
    last_rows, came_back = together(last_rows, came_back)
    middle = jnp.concatenate(
        [
            blocks_of(middle_rows[:, : 3 * width], 3),
            blocks_of(middle_rows[:, 3 * width : 4 * width], 1),
            blocks_of(middle_rows[:, 4 * width : 5 * width], 1),
            middle_rows[:, 5 * width :].reshape(tp, drow, part),
        ],
        axis=2,
    )
    middle = line_total(line_scatter(middle))
    last = jnp.concatenate(
        [
            blocks_of(last_rows[:, : 3 * width], 3),
            last_rows[:, 3 * width :].reshape(tp, drow, 256 // tp),
        ],
        axis=2,
    )
    last = line_total(line_scatter(last))
    grad_clips = (plain_first + dot_tn(pick_plain, came_back)).reshape(slots, tokens, width)
    grad_qkv = jnp.stack([last[:, : 3 * part], middle[:, : 3 * part]]).reshape(2, drow, 3, part)
    grad_proj = jnp.stack([middle[:, 4 * part : 5 * part].T, middle[:, 3 * part : 4 * part].T])
    grad_tfc = middle[:, 5 * part :].reshape(srow, width)
    smalls = last[:, 3 * part :].reshape(srow, 256)
    features = smalls[:, :14].T
    return (
        outputs,
        grad_clips,
        grad_qkv,
        grad_proj,
        line_total(fc1_parts),
        line_total(fc2_parts).T,
        features[10:14].reshape(attn_bias.shape),
        smalls[:1, 128 : 128 + drow],
        features[:6].reshape(3, 2, srow),
        grad_tfc,
        features[6:10],
    )


def solution(mesh):
    return jax.shard_map(
        shards,
        mesh=mesh,
        in_specs=(
            P("dp", "tensor", None),
            P("dp"),
            P(None, "dp", None, "tensor"),
            P(None, "tensor", "dp"),
            P("dp", "tensor"),
            P("tensor", "dp"),
            P(None, None, "tensor", "dp"),
            P("tensor", "dp"),
            P(None, None, ("dp", "tensor")),
            P(("dp", "tensor"), None),
            P(None, ("dp", "tensor")),
            P("dp", "tensor", None),
        ),
        out_specs=(
            P("dp", "tensor", None),
            P("dp", "tensor", None),
            P(None, "dp", None, "tensor"),
            P(None, "tensor", "dp"),
            P("dp", "tensor"),
            P("tensor", "dp"),
            P(None, None, "tensor", "dp"),
            P("tensor", "dp"),
            P(None, None, ("dp", "tensor")),
            P(("dp", "tensor"), None),
            P(None, ("dp", "tensor")),
        ),
        check_vma=False,
    )
```
